32 devices in a mesh: src: 4 (over y, x), snk: 4 (over z), slab: 2 (over core).
Axes of the slice: x: 2, y: 2, z: 4, core: 2. Of those that a mesh axis runs over, the one named last changes fastest.
Arguments:
- eigvecs: bfloat16 [8, 8192, 384], P('snk', ('src', 'slab')), may hold values from -0.125 to 0.125
- perambulator: bfloat16 [8, 8, 4, 192, 384], P('snk', 'src'), may hold values from -0.4375 to 0.4375
- momenta: int32 [4, 3], replicated, may hold values from 1 to 3
- source_times: int32 [8], P('src'), may hold values from 0 to 7, as said below
Outputs:
- blocks: float32 [4, 8, 8, 4, 192, 384], P(None, 'snk', 'src', None, 'slab')
The draws below stay inside these ranges and needn't reach their ends.
Inputs may be any that keep to these rules, and one draw needn't show every extreme that they name: `source_times`: distinct time slices.
All inputs are finite; a program needn't handle non-finite values.
Results may differ from the reference program's by a relative error of at most 0.0062.
Values may be sent and summed in bfloat16 or wider, within the bound.
No kernel may reach another device: no remote copies, remote signals or barrier semaphores. Data moves between devices by JAX's collectives and lax.ppermute only.
A program may use at most 128 MiB of HBM per device.

```python
import math
import jax
import jax.numpy as jnp

LX = 32
LY = 32
NEV = 192
NMOM = 4
LZ = 8
NSITE = 8192
NT = 8
NSRC = 8


def draw_source_times(key, part):
    order = jax.random.permutation(jax.random.fold_in(key, 11), NT)
    return order[:NSRC].astype(jnp.int32)


def place_ends(result, own_key, least, top_value):
    index_at = [jax.random.randint(jax.random.fold_in(own_key, axis), (), 0, length) for axis, length in enumerate(result.shape)]
    main_axis = result.shape.index(max(result.shape))
    neighbour = index_at[:main_axis] + [(index_at[main_axis] + 1) % result.shape[main_axis]] + index_at[main_axis + 1:]
    return result.at[tuple(index_at)].set(least).at[tuple(neighbour)].set(top_value)


def levels(key, extent, shards, low, largest):
    factor_of, own = 1.0, jax.random.fold_in(key, 6)
    for dim, parts in shards:
        heights = jnp.exp(jax.random.uniform(jax.random.fold_in(own, dim), (parts,), jnp.float32, low / len(shards), largest / len(shards)))
        factor_of = factor_of * jnp.repeat(heights, extent[dim] // parts).reshape([-1 if axis == dim else 1 for axis in range(len(extent))])
    return factor_of


def scatter_about(own_key, dims, deviation, bound, shards=(), held_as=jnp.bfloat16):
    factor_of = levels(own_key, dims, shards, -0.22, 0.18) if shards else 1.0
    drawn = jax.random.normal(own_key, dims, jnp.float32) * deviation * factor_of
    return jnp.minimum(jnp.maximum(drawn, -bound), bound).astype(held_as)


def setup_inputs(seed: int = 0) -> dict:
    key_list = jax.random.split(jax.random.key(seed), 5)
    return {
        "eigvecs": scatter_about(key_list[0], (NT, NSITE, 2 * NEV), (0.22 / NSITE ** 0.25), 0.125, ((0, 4), (1, 8))),
        "perambulator": scatter_about(key_list[1], (NT, NSRC, 4, NEV, 2 * NEV), NEV ** -0.5, 0.4375, ((0, 4), (1, 4))),
        "momenta": place_ends(jax.random.randint(key_list[2], (NMOM, 3), 1, 4), jax.random.fold_in(key_list[2], 1), 1, 3).astype(jnp.int32),
        "source_times": draw_source_times(jax.random.fold_in(key_list[4], 71), 0),
    }


def angles(momenta, xs, ys, zs, lz):
    fx = ((momenta[:, 0:1] * xs[None, :]) % LX).astype(jnp.float32) / LX
    fy = ((momenta[:, 1:2] * ys[None, :]) % LY).astype(jnp.float32) / LY
    fz = ((momenta[:, 2:3] * zs[None, :]) % lz).astype(jnp.float32) / lz
    return (2.0 * math.pi) * (fx + fy + fz)


def elemental(vec, angle):
    nev = vec.shape[1] // 2
    vf = vec.astype(jnp.float32)
    cosine = jnp.cos(angle)[:, None]
    sine = jnp.sin(angle)[:, None]
    vreal, vimag = vf[:, :nev], vf[:, nev:]
    phased = jnp.concatenate([cosine * vreal + sine * vimag, cosine * vimag - sine * vreal], axis=1).astype(jnp.bfloat16)
    gram = jnp.dot(vf.T, phased.astype(jnp.float32), preferred_element_type=jnp.float32)
    real = gram[:nev, :nev] + gram[nev:, nev:]
    imag = gram[:nev, nev:] - gram[nev:, :nev]
    return jnp.concatenate([real, imag], axis=1)


def reference(eigvecs, perambulator, momenta, source_times):
    nev = NEV
    sites = jnp.arange(NSITE, dtype=jnp.int32)
    xs = sites % LX
    ys = (sites // LX) % LY
    zs = sites // (LX * LY)
    angle = angles(momenta, xs, ys, zs, LZ)
    slices = []
    for t in range(NT):
        per_mom = [elemental(eigvecs[t], angle[m]) for m in range(NMOM)]
        slices.append(jnp.stack(per_mom, axis=0))
    phi = jnp.stack(slices, axis=0).astype(jnp.bfloat16)
    source = phi[source_times]
    tau = perambulator.astype(jnp.float32)
    outs = []
    for m in range(NMOM):
        sink = phi[:, m].astype(jnp.float32)
        stacked = jnp.concatenate([sink[:, :, :nev], sink[:, :, nev:]], axis=1)
        prod = jnp.einsum('tra,tsqab->tsqrb', stacked, tau)
        creal = prod[..., :nev, :nev] - prod[..., nev:, nev:]
        cimag = prod[..., :nev, nev:] + prod[..., nev:, :nev]
        half = jnp.concatenate([creal, cimag], axis=3).astype(jnp.bfloat16).astype(jnp.float32)
        src = source[:, m].astype(jnp.float32)
        both = jnp.concatenate([src[:, :, :nev], src[:, :, nev:]], axis=1)
        quad = jnp.einsum('tsqrb,scb->tsqrc', half, both)
        dreal = quad[..., :nev, :nev] + quad[..., nev:, nev:]
        dimag = quad[..., nev:, :nev] - quad[..., :nev, nev:]
        outs.append(jnp.concatenate([dreal, dimag], axis=-1))
    return jnp.stack(outs, axis=0)
```

```python
import functools
import math

import jax
import jax.numpy as jnp
from jax import lax
from jax.experimental import pallas as pl
from jax.experimental.pallas import tpu as pltpu
from jax.sharding import PartitionSpec as P

LX = 32
LY = 32
TAIL = 16
F32 = jnp.float32
BF16 = jnp.bfloat16
VMEM = pl.BlockSpec(memory_space=pltpu.VMEM)
SMEM = pl.BlockSpec(memory_space=pltpu.SMEM)


def angles(momenta, xs, ys, zs, lz):
    fx = (momenta[:, 0:1] * xs[None, :] % LX).astype(F32) / LX
    fy = (momenta[:, 1:2] * ys[None, :] % LY).astype(F32) / LY
    fz = (momenta[:, 2:3] * zs[None, :] % lz).astype(F32) / lz
    return 2.0 * math.pi * (fx + fy + fz)


def general(eigvecs, perambulator, momenta, source_times):
    nev = eigvecs.shape[2] // 2
    count = eigvecs.shape[1]
    zpl = count // (LX * LY)
    slabs = lax.axis_size("slab")
    lz = zpl * lax.axis_size("src") * slabs
    sites = jnp.arange(count, dtype=jnp.int32)
    xs = sites % LX
    ys = sites // LX % LY
    zs = sites // (LX * LY) + lax.axis_index(("src", "slab")) * zpl
    angle = angles(momenta, xs, ys, zs, lz)
    vreal = eigvecs[:, :, :nev].astype(F32)
    vimag = eigvecs[:, :, nev:].astype(F32)
    partials = []
    for m in range(angle.shape[0]):
        cosine = jnp.cos(angle[m])[None, :, None]
        sine = jnp.sin(angle[m])[None, :, None]
        phased = jnp.concatenate(
            [cosine * vreal + sine * vimag, cosine * vimag - sine * vreal], axis=2
        ).astype(BF16)
        gram = jnp.einsum("tsa,tsb->tab", eigvecs, phased, preferred_element_type=F32)
        real = gram[:, :nev, :nev] + gram[:, nev:, nev:]
        imag = gram[:, :nev, nev:] - gram[:, nev:, :nev]
        partials.append(jnp.concatenate([real, imag], axis=2))
    partial_value = jnp.stack(partials, axis=1)
    tdev = partial_value.shape[0]
    rows = nev // slabs
    local_times = lax.axis_index("snk") * tdev + jnp.arange(tdev, dtype=jnp.int32)
    slab_part = lax.psum_scatter(partial_value, "slab", scatter_dimension=2, tiled=True)
    share = lax.psum_scatter(slab_part, "src", scatter_dimension=2, tiled=True).astype(BF16)
    sink = lax.all_gather(share, "src", axis=2, tiled=True)
    selector = (source_times[:, None] == local_times[None, :]).astype(BF16)
    term = jnp.dot(selector, sink.reshape(tdev, -1), preferred_element_type=F32)
    picked = lax.psum(term.astype(BF16), "snk")
    picked = picked.reshape((source_times.shape[0],) + sink.shape[1:])
    source = lax.all_gather(picked, "slab", axis=2, tiled=True)
    stacked = jnp.concatenate([sink[..., :nev], sink[..., nev:]], axis=2)
    prod = jnp.einsum("tmra,tsqab->mtsqrb", stacked, perambulator, preferred_element_type=F32)
    creal = prod[..., :rows, :nev] - prod[..., rows:, nev:]
    cimag = prod[..., :rows, nev:] + prod[..., rows:, :nev]
    half = jnp.concatenate([creal, cimag], axis=4).astype(BF16)
    both = jnp.concatenate([source[..., :nev], source[..., nev:]], axis=2)
    quad = jnp.einsum("mtsqrb,smcb->mtsqrc", half, both, preferred_element_type=F32)
    dreal = quad[..., :rows, :nev] + quad[..., rows:, nev:]
    dimag = quad[..., rows:, :nev] - quad[..., :rows, nev:]
    return jnp.concatenate([dreal, dimag], axis=-1)


def turned(x, nev):
    return jnp.concatenate([x[:, nev:], -x[:, :nev]], axis=1)


def gram_kernel(nsrc, slabs, lz, sibling, mom_ref, eig_ref, *refs):
    if sibling:
        acc_in, times_ref = refs[:2]
        outs = refs[2 : 2 + nsrc]
        tab, turn, wide, tran, acc = refs[2 + nsrc :]
    else:
        (acc_out,) = refs[:1]
        tab, turn, wide, tran, acc = refs[1:]
    times, count, width = eig_ref.shape
    nev = width // 2
    rows = nev // slabs
    src = lax.axis_index("src")
    slab = lax.axis_index("slab")
    z = src * slabs + (1 - slab if sibling else slab)
    index = lax.broadcasted_iota(jnp.int32, (LX, 128), 0)
    for k in range(nsrc):
        m = src ^ k
        ax = (2.0 * math.pi) * ((mom_ref[m, 0] * index % LX).astype(F32) / LX)
        fz = (mom_ref[m, 2] * z % lz).astype(F32) / lz
        ay = (2.0 * math.pi) * ((mom_ref[m, 1] * index % LY).astype(F32) / LY + fz)
        tab[0, k] = jnp.cos(ax)
        tab[1, k] = jnp.sin(ax)
        tab[2, k] = jnp.cos(ay)
        tab[3, k] = jnp.sin(ay)
    wides = width // 128
    for t in range(times):
        tran[...] = eig_ref[t].T

        def phase(y, _):
            at = pl.multiple_of(y * LX, LX)
            v = eig_ref[t, pl.ds(at, LX), :].astype(F32)
            u = turned(v, nev)
            for k in range(nsrc):
                cy = jnp.broadcast_to(tab[2, k, pl.ds(y, 1), :], (LX, 128))
                sy = jnp.broadcast_to(tab[3, k, pl.ds(y, 1), :], (LX, 128))
                cx, sx = tab[0, k], tab[1, k]
                c = cx * cy - sx * sy
                s = sx * cy + cx * sy
                c = jnp.concatenate([c] * wides, axis=1)
                s = jnp.concatenate([s] * wides, axis=1)
                wide[pl.ds(at, LX), k * width : (k + 1) * width] = (c * v + s * u).astype(BF16)
            return 0

        lax.fori_loop(0, count // LX, phase, 0)
        at_r = pl.multiple_of(slab * rows, rows)
        at_i = pl.multiple_of(slab * rows + nev, rows)
        for k in range(nsrc):
            w = wide[:, k * width : (k + 1) * width]
            up = jnp.dot(tran[pl.ds(at_r, rows), :], w, preferred_element_type=F32)
            lo = jnp.dot(tran[pl.ds(at_i, rows), :], w, preferred_element_type=F32)
            e = up + turned(lo, nev)
            if sibling:
                e = e + acc_in[k, t]
                if k == 0:
                    outs[0][t] = e
                else:
                    outs[k][t, :rows, :] = e.astype(BF16)
                    outs[k][t, rows:, :] = jnp.full((TAIL, width), times_ref[t].astype(F32), F32).astype(BF16)
            else:
                acc_out[k, t] = e


def sum_kernel(own, *refs):
    out = refs[-1]
    rows = own.shape[1]
    total = own[...]
    for r in refs[:-1]:
        total = total + r[:, :rows, :].astype(F32)
    out[...] = total.astype(BF16)


def pick_kernel(nsnk, nsrc, times_ref, *refs):
    sent = refs[: nsrc - 1]
    seen = refs[nsrc - 1 : nsrc - 1 + nsnk]
    outs = refs[nsrc - 1 + nsnk :]
    tdev, rows, width = seen[0].shape
    snk = lax.axis_index("snk")
    for k in range(nsrc):
        for s in range(outs[k].shape[0]):
            if k == 0:
                want = jnp.full((TAIL, width), times_ref[s].astype(F32), F32)
            else:
                want = sent[k - 1][s, rows:, :].astype(F32)
            mask = []
            for d in range(nsnk):
                for t in range(tdev):
                    time = (lax.rem(snk + nsnk - d, nsnk) * tdev + t).astype(F32)
                    mask.append((want == time).astype(F32))
            for r in range(rows // TAIL):
                total = jnp.zeros((TAIL, width), F32)
                for d in range(nsnk):
                    for t in range(tdev):
                        total = total + mask[d * tdev + t] * seen[d][t, r * TAIL : (r + 1) * TAIL, :].astype(F32)
                outs[k][s, r * TAIL : (r + 1) * TAIL, :] = total.astype(BF16)


def half_kernel(nsrc, *refs):
    sinks = refs[:nsrc]
    per_ref, out_ref, lhs = refs[nsrc:]
    rows, width = sinks[0].shape[1:]
    nev = width // 2
    for k in range(nsrc):
        lhs[k * rows : (k + 1) * rows, :] = sinks[k][0]
    p = per_ref[0, 0, 0].astype(F32)
    q = -turned(p, nev)
    both = jnp.concatenate([p, q], axis=0).astype(BF16)
    h = jnp.dot(lhs[...], both, preferred_element_type=F32).astype(BF16)
    for k in range(nsrc):
        out_ref[k, 0, 0] = h[k * rows : (k + 1) * rows, :]


def block_kernel(nsrc, index_ref, half_ref, *refs):
    del index_ref
    mine = refs[:nsrc]
    other = refs[nsrc : 2 * nsrc]
    out_ref, rhs = refs[2 * nsrc :]
    rows, width = mine[0].shape[1:]
    nev = width // 2
    slab = lax.axis_index("slab")
    k = pl.program_id(0)
    for j in range(nsrc):

        @pl.when(k == j)
        def _():
            rhs[pl.ds(pl.multiple_of(slab * rows, rows), rows), :] = mine[j][0]
            rhs[pl.ds(pl.multiple_of((1 - slab) * rows, rows), rows), :] = other[j][0]

    rhs[nev:, :] = (-turned(rhs[:nev, :].astype(F32), nev)).astype(BF16)
    shape = half_ref.shape
    lhs = half_ref[0, 0].reshape(shape[2] * rows, width)
    out = lax.dot_general(lhs, rhs[...], (((1,), (1,)), ((), ())), preferred_element_type=F32)
    out_ref[...] = out.reshape(out_ref.shape)


def fast(eigvecs, perambulator, momenta, source_times):
    nsrc, nsnk, slabs = (lax.axis_size(a) for a in ("src", "snk", "slab"))
    tdev, count, width = eigvecs.shape
    sdev = source_times.shape[0]
    nq = perambulator.shape[2]
    nev = width // 2
    rows = nev // slabs
    lz = count // (LX * LY) * nsrc * slabs
    src = lax.axis_index("src")

    def swap(x):
        return lax.ppermute(x, "slab", [(0, 1), (1, 0)])

    def cross(x, k):
        return lax.ppermute(x, "src", [(i, i ^ k) for i in range(nsrc)])

    def shift(x, d):
        return lax.ppermute(x, "snk", [(i, (i + d) % nsnk) for i in range(nsnk)])

    scratch = [
        pltpu.VMEM((4, nsrc, LX, 128), F32),
        pltpu.VMEM((8, 128), F32),
        pltpu.VMEM((count, nsrc * width), BF16),
        pltpu.VMEM((width, count), BF16),
        pltpu.VMEM((8, 128), F32),
    ]
    gram_cost = pl.CostEstimate(
        flops=2 * tdev * count * 2 * rows * width * nsrc, bytes_accessed=2 * eigvecs.size, transcendentals=0
    )
    theirs = swap(eigvecs)
    acc = pl.pallas_call(
        functools.partial(gram_kernel, nsrc, slabs, lz, False),
        out_shape=jax.ShapeDtypeStruct((nsrc, tdev, rows, width), F32),
        in_specs=[SMEM, VMEM],
        out_specs=VMEM,
        scratch_shapes=scratch,
        cost_estimate=gram_cost,
        name="gram_own",
    )(momenta, eigvecs)
    pieces = pl.pallas_call(
        functools.partial(gram_kernel, nsrc, slabs, lz, True),
        out_shape=[jax.ShapeDtypeStruct((tdev, rows, width), F32)]
        + [jax.ShapeDtypeStruct((tdev, rows + TAIL, width), BF16)] * (nsrc - 1),
        in_specs=[SMEM, VMEM, VMEM, SMEM],
        out_specs=[VMEM] * nsrc,
        scratch_shapes=scratch,
        cost_estimate=gram_cost,
        name="gram_sibling",
    )(momenta, theirs, acc, source_times)
    got = [cross(pieces[k], k) for k in range(1, nsrc)]
    red = pl.pallas_call(
        sum_kernel,
        out_shape=jax.ShapeDtypeStruct((tdev, rows, width), BF16),
        in_specs=[VMEM] * nsrc,
        out_specs=VMEM,
        name="sum",
    )(pieces[0], *got)
    seen = [red] + [shift(red, d) for d in range(1, nsnk)]
    sinks = [red] + [cross(red, k) for k in range(1, nsrc)]
    picked = pl.pallas_call(
        functools.partial(pick_kernel, nsnk, nsrc),
        out_shape=[jax.ShapeDtypeStruct((sdev, rows, width), BF16)] * nsrc,
        in_specs=[SMEM] + [VMEM] * (nsrc - 1 + nsnk),
        out_specs=[VMEM] * nsrc,
        name="pick",
    )(source_times, *got, *seen)
    mine = [picked[0]] + [cross(picked[k], k) for k in range(1, nsrc)]
    other = [swap(x) for x in mine]

    tq = tdev * nq
    whole = pl.BlockSpec((1, rows, width), lambda t, s, q: (t, 0, 0))
    half = pl.pallas_call(
        functools.partial(half_kernel, nsrc),
        out_shape=jax.ShapeDtypeStruct((nsrc, sdev, tq, rows, width), BF16),
        grid=(tdev, sdev, nq),
        in_specs=[whole] * nsrc
        + [pl.BlockSpec((1, 1, 1, nev, width), lambda t, s, q: (t, s, q, 0, 0))],
        out_specs=pl.BlockSpec((nsrc, 1, 1, rows, width), lambda t, s, q: (0, s, t * nq + q, 0, 0)),
        scratch_shapes=[pltpu.VMEM((nsrc * rows, width), BF16)],
        cost_estimate=pl.CostEstimate(
            flops=4 * tq * sdev * nsrc * rows * width * width // 2,
            bytes_accessed=2 * perambulator.size,
            transcendentals=0,
        ),
        name="half",
    )(*sinks, perambulator)
    spec = pl.BlockSpec((1, rows, width), lambda k, s, i: (s, 0, 0))
    blocks = pl.pallas_call(
        functools.partial(block_kernel, nsrc),
        out_shape=jax.ShapeDtypeStruct((nsrc, tdev, sdev, nq, rows, width), F32),
        grid_spec=pltpu.PrefetchScalarGridSpec(
            num_scalar_prefetch=1,
            grid=(nsrc, sdev),
            in_specs=[pl.BlockSpec((1, 1, tq, rows, width), lambda k, s, i: (k, s, 0, 0, 0))]
            + [spec] * (2 * nsrc),
            out_specs=pl.BlockSpec(
                (1, tdev, 1, nq, rows, width), lambda k, s, i: (i[0] ^ k, 0, s, 0, 0, 0)
            ),
            scratch_shapes=[pltpu.VMEM((width, width), BF16)],
        ),
        name="blocks",
    )(src.astype(jnp.int32).reshape(1), half, *mine, *other)
    return blocks


def local(eigvecs, perambulator, momenta, source_times):
    nsrc = lax.axis_size("src")
    fits = (
        lax.axis_size("slab") == 2
        and momenta.shape[0] == nsrc
        and nsrc & (nsrc - 1) == 0
        and eigvecs.shape[1] == LX * LY
        and source_times.shape[0] == eigvecs.shape[0]
    )
    return (fast if fits else general)(eigvecs, perambulator, momenta, source_times)


def solution(mesh):
    placed = (P("snk", ("src", "slab"), None), P("snk", "src", None, None, None), P(), P("src"))
    return jax.shard_map(
        local,
        mesh=mesh,
        in_specs=placed,
        out_specs=P(None, "snk", "src", None, "slab", None),
        check_vma=False,
    )
```

```python
import functools
import math

import jax
import jax.numpy as jnp
from jax import lax
from jax.experimental import pallas as pl
from jax.experimental.pallas import tpu as pltpu
from jax.sharding import PartitionSpec as P


LX = 32
LY = 32
TAIL = 16
F32 = jnp.float32
BF16 = jnp.bfloat16
VMEM = pl.BlockSpec(memory_space=pltpu.VMEM)
SMEM = pl.BlockSpec(memory_space=pltpu.SMEM)


def angles(momenta, xs, ys, zs, lz):
    fx = (momenta[:, 0:1] * xs[None, :] % LX).astype(F32) / LX
    fy = (momenta[:, 1:2] * ys[None, :] % LY).astype(F32) / LY
    fz = (momenta[:, 2:3] * zs[None, :] % lz).astype(F32) / lz
    return 2.0 * math.pi * (fx + fy + fz)


def general(eigvecs, perambulator, momenta, source_times):
    nev = eigvecs.shape[2] // 2
    count = eigvecs.shape[1]
    zpl = count // (LX * LY)
    slabs = lax.axis_size("slab")
    lz = zpl * lax.axis_size("src") * slabs
    sites = jnp.arange(count, dtype=jnp.int32)
    xs = sites % LX
    ys = sites // LX % LY
    zs = sites // (LX * LY) + lax.axis_index(("src", "slab")) * zpl
    angle = angles(momenta, xs, ys, zs, lz)
    vreal = eigvecs[:, :, :nev].astype(F32)
    vimag = eigvecs[:, :, nev:].astype(F32)
    partials = []
    for m in range(angle.shape[0]):
        cosine = jnp.cos(angle[m])[None, :, None]
        sine = jnp.sin(angle[m])[None, :, None]
        phased = jnp.concatenate(
            [cosine * vreal + sine * vimag, cosine * vimag - sine * vreal], axis=2
        ).astype(BF16)
        gram = jnp.einsum("tsa,tsb->tab", eigvecs, phased, preferred_element_type=F32)
        real = gram[:, :nev, :nev] + gram[:, nev:, nev:]
        imag = gram[:, :nev, nev:] - gram[:, nev:, :nev]
        partials.append(jnp.concatenate([real, imag], axis=2))
    partial_value = jnp.stack(partials, axis=1)
    tdev = partial_value.shape[0]
    rows = nev // slabs
    local_times = lax.axis_index("snk") * tdev + jnp.arange(tdev, dtype=jnp.int32)
    slab_part = lax.psum_scatter(partial_value, "slab", scatter_dimension=2, tiled=True)
    share = lax.psum_scatter(slab_part, "src", scatter_dimension=2, tiled=True).astype(BF16)
    sink = lax.all_gather(share, "src", axis=2, tiled=True)
    selector = (source_times[:, None] == local_times[None, :]).astype(BF16)
    term = jnp.dot(selector, sink.reshape(tdev, -1), preferred_element_type=F32)
    picked = lax.psum(term.astype(BF16), "snk")
    picked = picked.reshape((source_times.shape[0],) + sink.shape[1:])
    source = lax.all_gather(picked, "slab", axis=2, tiled=True)
    stacked = jnp.concatenate([sink[..., :nev], sink[..., nev:]], axis=2)
    prod = jnp.einsum("tmra,tsqab->mtsqrb", stacked, perambulator, preferred_element_type=F32)
    creal = prod[..., :rows, :nev] - prod[..., rows:, nev:]
    cimag = prod[..., :rows, nev:] + prod[..., rows:, :nev]
    half = jnp.concatenate([creal, cimag], axis=4).astype(BF16)
    both = jnp.concatenate([source[..., :nev], source[..., nev:]], axis=2)
    quad = jnp.einsum("mtsqrb,smcb->mtsqrc", half, both, preferred_element_type=F32)
    dreal = quad[..., :rows, :nev] + quad[..., rows:, nev:]
    dimag = quad[..., rows:, :nev] - quad[..., :rows, nev:]
    return jnp.concatenate([dreal, dimag], axis=-1)


def turned(x, nev):
    return jnp.concatenate([x[:, nev:], -x[:, :nev]], axis=1)


def circle(f):
    turns = jnp.floor(4.0 * f + 0.5)
    r = (f - 0.25 * turns) * (2.0 * math.pi)
    n = turns.astype(jnp.int32) & 3
    x = r * r
    c = 1.0 + x * (-1 / 2 + x * (1 / 24 + x * (-1 / 720 + x * (1 / 40320))))
    s = r * (1.0 + x * (-1 / 6 + x * (1 / 120 + x * (-1 / 5040 + x * (1 / 362880)))))
    odd = (n & 1) == 1
    cosine = jnp.where(odd, s, c)
    sine = jnp.where(odd, c, s)
    return (
        jnp.where((n == 1) | (n == 2), -cosine, cosine),
        jnp.where(n >= 2, -sine, sine),
    )


def phases(pieces, z, lz, mom_ref, tab):
    src = lax.axis_index("src")
    index = lax.broadcasted_iota(jnp.int32, (LX, 128), 0)
    for i, k in enumerate(pieces):
        m = src ^ k
        tab[0, i], tab[1, i] = circle((mom_ref[m, 0] * index % LX).astype(F32) / LX)
        fz = (mom_ref[m, 2] * z % lz).astype(F32) / lz
        tab[2, i], tab[3, i] = circle((mom_ref[m, 1] * index % LY).astype(F32) / LY + fz)


def spread(pieces, vec, tab, wide):
    count, width = vec.shape
    nev = width // 2

    def step(y, _):
        at = pl.multiple_of(y * LX, LX)
        v = vec[pl.ds(at, LX), :].astype(F32)
        u = turned(v, nev)
        for i in range(len(pieces)):
            cy = jnp.broadcast_to(tab[2, i, pl.ds(y, 1), :], (LX, 128))
            sy = jnp.broadcast_to(tab[3, i, pl.ds(y, 1), :], (LX, 128))
            cx, sx = tab[0, i], tab[1, i]
            c = jnp.concatenate([cx * cy - sx * sy] * (width // 128), axis=1)
            s = jnp.concatenate([sx * cy + cx * sy] * (width // 128), axis=1)
            wide[pl.ds(at, LX), i * width : (i + 1) * width] = (c * v + s * u).astype(BF16)
        return 0

    lax.fori_loop(0, count // LX, step, 0, unroll=2)


def gather_rows(pieces, vec, tab, wide, tran, add):
    width = vec.shape[1]
    nev = width // 2
    spread(pieces, vec, tab, wide)
    tran[...] = vec[...].T
    for i, k in enumerate(pieces):
        g = jnp.dot(tran[...], wide[:, i * width : (i + 1) * width], preferred_element_type=F32)
        add(i, k, g[:nev] + turned(g[nev:], nev))


def own_kernel(slabs, lz, pieces, mom_hbm, eig_hbm, acc_ref, vec, tab, wide, tran, mom_ref, sem):
    slab = lax.axis_index("slab")
    small = pltpu.make_async_copy(mom_hbm, mom_ref, sem.at[0])
    large = pltpu.make_async_copy(eig_hbm.at[slab], vec, sem.at[1])
    small.start()
    large.start()
    small.wait()
    phases(pieces, lax.axis_index("src") * slabs + slab, lz, mom_ref, tab)
    large.wait()

    def add(i, k, sums):
        acc_ref[i] = sums

    gather_rows(pieces, vec, tab, wide, tran, add)


def sibling_kernel(slabs, lz, pieces, mom_hbm, times_hbm, eig_ref, acc_ref, *refs):
    outs = refs[: len(pieces)]
    tab, wide, tran, mom_ref, times_ref, sem = refs[len(pieces) :]
    width = eig_ref.shape[2]
    nev = width // 2
    slab = lax.axis_index("slab")
    small = pltpu.make_async_copy(mom_hbm, mom_ref, sem.at[0])
    times = pltpu.make_async_copy(times_hbm, times_ref, sem.at[1])
    small.start()
    times.start()
    small.wait()
    phases(pieces, lax.axis_index("src") * slabs + 1 - slab, lz, mom_ref, tab)

    def add(i, k, sums):
        outs[i][:nev, :] = (sums + acc_ref[i]).astype(BF16)

    gather_rows(pieces, eig_ref.at[slab], tab, wide, tran, add)
    times.wait()
    for i in range(len(pieces)):
        for s in range(times_ref.shape[0]):
            time = jnp.full((TAIL, width), times_ref[s].astype(F32), F32)
            outs[i][nev + s * TAIL : nev + (s + 1) * TAIL, :] = time.astype(BF16)


def last_kernel(slabs, lz, mom_hbm, eig_hbm, eig_ref, out, vec, tab, wide, tran, mom_ref, sem):
    slab = lax.axis_index("slab")
    src = lax.axis_index("src")
    small = pltpu.make_async_copy(mom_hbm, mom_ref, sem.at[0])
    large = pltpu.make_async_copy(eig_hbm.at[slab], vec, sem.at[1])
    small.start()
    large.start()
    small.wait()
    phases([0], src * slabs + 1 - slab, lz, mom_ref, tab)

    def put(i, k, sums):
        out[...] = sums

    gather_rows([0], eig_ref.at[slab], tab, wide, tran, put)
    phases([0], src * slabs + slab, lz, mom_ref, tab)
    large.wait()

    def add(i, k, sums):
        out[...] = out[...] + sums

    gather_rows([0], vec, tab, wide, tran, add)


def sum_kernel(own, *refs):
    keep, send = refs[-2:]
    rows = keep.shape[0]
    slab = lax.axis_index("slab")
    for out, part in ((keep, slab), (send, 1 - slab)):
        at = pl.multiple_of(part * rows, rows)
        total = own[pl.ds(at, rows), :]
        for r in refs[:-2]:
            total = total + r[pl.ds(at, rows), :].astype(F32)
        out[...] = total.astype(BF16)


def join_kernel(keep, came, out):
    slab = lax.axis_index("slab")
    out[slab] = keep[...]
    out[1 - slab] = came[...]


def pick_kernel(nsnk, nsrc, times_ref, *refs):
    sent = refs[: nsrc - 1]
    seen = refs[nsrc - 1 : nsrc - 1 + nsnk]
    outs = refs[nsrc - 1 + nsnk :]
    tdev, rows, width = seen[0].shape
    nev = width // 2
    snk = lax.axis_index("snk")
    for k in range(nsrc):
        for s in range(outs[k].shape[0]):
            if k == 0:
                want = jnp.full((TAIL, 128), times_ref[s].astype(F32), F32)
            else:
                want = sent[k - 1][nev + s * TAIL : nev + (s + 1) * TAIL, :128].astype(F32)
            mask = []
            for d in range(nsnk):
                for t in range(tdev):
                    time = ((snk ^ d) * tdev + t).astype(F32)
                    one = (want == time).astype(F32).astype(BF16)
                    mask.append(jnp.concatenate([one] * (width // 128), axis=1))
            for r in range(rows // TAIL):
                total = None
                for d in range(nsnk):
                    for t in range(tdev):
                        term = mask[d * tdev + t] * seen[d][t, r * TAIL : (r + 1) * TAIL, :]
                        total = term if total is None else total + term
                outs[k][s, r * TAIL : (r + 1) * TAIL, :] = total


def half_kernel(nsrc, *refs):
    sinks = refs[:nsrc]
    per_ref, out_ref, lhs, rhs = refs[nsrc:]
    rows, width = sinks[0].shape[1:]
    nev = width // 2
    nq = per_ref.shape[2]
    for k in range(nsrc):
        lhs[k * rows : (k + 1) * rows, :] = sinks[k][0]
    for q in range(nq):
        p = per_ref[0, 0, q]
        rhs[:nev, q * width : (q + 1) * width] = p
        rhs[nev:, q * width : (q + 1) * width] = (-turned(p.astype(F32), nev)).astype(BF16)
    h = jnp.dot(lhs[...], rhs[...], preferred_element_type=F32).astype(BF16)
    for q in range(nq):
        for k in range(nsrc):
            out_ref[k, 0, q] = h[k * rows : (k + 1) * rows, q * width : (q + 1) * width]


def block_kernel(pieces, index_ref, half_ref, *refs):
    del index_ref
    mine = refs[:pieces]
    other = refs[pieces : 2 * pieces]
    out_ref, rhs = refs[-2:]
    rows, width = mine[0].shape[1:]
    nev = width // 2
    slab = lax.axis_index("slab")
    for j in range(pieces):

        @pl.when((pl.program_id(0) == j) & (pl.program_id(2) == 0))
        def _():
            rhs[pl.ds(pl.multiple_of(slab * rows, rows), rows), :] = mine[j][0]
            rhs[pl.ds(pl.multiple_of((1 - slab) * rows, rows), rows), :] = other[j][0]
            rhs[nev:, :] = (-turned(rhs[:nev, :].astype(F32), nev)).astype(BF16)

    nq = half_ref.shape[2]
    lhs = half_ref[0, 0].reshape(nq * rows, width)
    out = lax.dot_general(lhs, rhs[...], (((1,), (1,)), ((), ())), preferred_element_type=F32)
    out_ref[...] = out.reshape(out_ref.shape)


def fast(eigvecs, perambulator, momenta, source_times):
    nsrc, nsnk, slabs = (lax.axis_size(a) for a in ("src", "snk", "slab"))
    tdev, count, width = eigvecs.shape
    sdev = source_times.shape[0]
    nq = perambulator.shape[2]
    nev = width // 2
    rows = nev // slabs
    lz = count // (LX * LY) * nsrc * slabs
    index = lax.axis_index("src").astype(jnp.int32).reshape(1)

    def shape(dims, dtype=BF16):
        return jax.ShapeDtypeStruct(dims, dtype)

    def params(mib):
        return pltpu.CompilerParams(vmem_limit_bytes=mib * 2**20)

    def cost(flops, moved):
        return pl.CostEstimate(flops=flops, bytes_accessed=moved, transcendentals=0)

    def swap(x):
        return lax.ppermute(x, "slab", [(0, 1), (1, 0)])

    def cross(x, k):
        return lax.ppermute(x, "src", [(i, i ^ k) for i in range(nsrc)])

    def along(x, d):
        return lax.ppermute(x, "snk", [(i, i ^ d) for i in range(nsnk)])

    theirs = swap(eigvecs)
    work = 2 * width * count * width
    hbm = pl.BlockSpec(memory_space=pltpu.HBM)
    sent = list(range(nsrc - 1, 0, -1))

    def grams(n, *more):
        return [
            pltpu.VMEM((4, n, LX, 128), F32),
            pltpu.VMEM((count, n * width), BF16),
            pltpu.VMEM((width, count), BF16),
            pltpu.SMEM(momenta.shape, jnp.int32),
            *more,
            pltpu.SemaphoreType.DMA((2,)),
        ]

    vec = pltpu.VMEM((count, width), BF16)
    acc = pl.pallas_call(
        functools.partial(own_kernel, slabs, lz, sent),
        out_shape=shape((len(sent), nev, width), F32),
        in_specs=[hbm, hbm],
        out_specs=VMEM,
        scratch_shapes=[vec] + grams(len(sent)),
        cost_estimate=cost(len(sent) * work, 2 * count * width),
        compiler_params=params(12),
        name="gram_own",
    )(momenta, eigvecs)
    parts = pl.pallas_call(
        functools.partial(sibling_kernel, slabs, lz, sent),
        out_shape=[shape((nev + sdev * TAIL, width))] * len(sent),
        in_specs=[hbm, hbm, VMEM, VMEM],
        out_specs=[VMEM] * len(sent),
        scratch_shapes=grams(len(sent), pltpu.SMEM(source_times.shape, jnp.int32)),
        cost_estimate=cost(len(sent) * work, 2 * count * width),
        compiler_params=params(12),
        name="gram_sibling",
    )(momenta, source_times, theirs, acc)
    got = [cross(part, k) for k, part in zip(sent, parts)][::-1]
    own = pl.pallas_call(
        functools.partial(last_kernel, slabs, lz),
        out_shape=shape((nev, width), F32),
        in_specs=[hbm, hbm, VMEM],
        out_specs=VMEM,
        scratch_shapes=[vec] + grams(1),
        cost_estimate=cost(2 * work, 2 * count * width),
        compiler_params=params(12),
        name="gram_last",
    )(momenta, eigvecs, theirs)
    keep, send = pl.pallas_call(
        sum_kernel,
        out_shape=[shape((rows, width))] * 2,
        in_specs=[VMEM] * nsrc,
        out_specs=[VMEM] * 2,
        compiler_params=params(4),
        name="sum",
    )(own, *got)
    red = pl.pallas_call(
        join_kernel,
        out_shape=shape((tdev, rows, width)),
        in_specs=[VMEM] * 2,
        out_specs=VMEM,
        compiler_params=params(4),
        name="join",
    )(keep, swap(send))
    seen = [red] + [along(red, d) for d in range(1, nsnk)]
    sinks = [red] + [cross(red, k) for k in range(1, nsrc)]
    picked = pl.pallas_call(
        functools.partial(pick_kernel, nsnk, nsrc),
        out_shape=[shape((sdev, rows, width))] * nsrc,
        in_specs=[SMEM] + [VMEM] * (nsrc - 1 + nsnk),
        out_specs=[VMEM] * nsrc,
        compiler_params=params(8),
        name="pick",
    )(source_times, *got, *seen)

    tq = tdev * nq
    per_t = pl.BlockSpec((1, rows, width), lambda t, s: (t, 0, 0))
    half = pl.pallas_call(
        functools.partial(half_kernel, nsrc),
        out_shape=shape((nsrc, sdev, tq, rows, width)),
        grid=(tdev, sdev),
        in_specs=[per_t] * nsrc
        + [pl.BlockSpec((1, 1, nq, nev, width), lambda t, s: (t, s, 0, 0, 0))],
        out_specs=pl.BlockSpec((nsrc, 1, nq, rows, width), lambda t, s: (0, s, t, 0, 0)),
        scratch_shapes=[
            pltpu.VMEM((nsrc * rows, width), BF16),
            pltpu.VMEM((width, nq * width), BF16),
        ],
        cost_estimate=cost(2 * tq * sdev * nsrc * rows * width * width, 2 * perambulator.size),
        compiler_params=params(16),
        name="half",
    )(*sinks, perambulator)

    mine = [picked[0]] + [cross(picked[k], k) for k in range(1, nsrc)]
    other = [swap(x) for x in mine]

    def finish(first, count, before):
        n = count
        chained = before is not None
        return pl.pallas_call(
            functools.partial(block_kernel, n),
            out_shape=shape((nsrc, tdev, sdev, nq, rows, width), F32),
            grid_spec=pltpu.PrefetchScalarGridSpec(
                num_scalar_prefetch=1,
                grid=(n, sdev, tdev),
                in_specs=[
                    pl.BlockSpec(
                        (1, 1, nq, rows, width), lambda k, s, t, i: (first + k, s, t, 0, 0)
                    )
                ]
                + [pl.BlockSpec((1, rows, width), lambda k, s, t, i: (s, 0, 0))] * (2 * n)
                + [pl.BlockSpec(memory_space=pl.ANY)] * chained,
                out_specs=pl.BlockSpec(
                    (1, 1, 1, nq, rows, width),
                    lambda k, s, t, i: (i[0] ^ (first + k), t, s, 0, 0, 0),
                ),
                scratch_shapes=[pltpu.VMEM((width, width), BF16)],
            ),
            input_output_aliases={2 + 2 * n: 0} if chained else {},
            cost_estimate=cost(
                2 * n * tq * sdev * rows * width * width, 4 * n * tq * sdev * rows * width
            ),
            compiler_params=params(12),
        )(
            index,
            half,
            *mine[first : first + n],
            *other[first : first + n],
            *([before] if chained else []),
        )

    blocks = finish(0, 1, None)
    return finish(1, nsrc - 1, blocks)


def local(eigvecs, perambulator, momenta, source_times):
    nsrc = lax.axis_size("src")
    fits = (
        lax.axis_size("slab") == 2
        and momenta.shape[0] == nsrc
        and nsrc & (nsrc - 1) == 0
        and eigvecs.shape[1] == LX * LY
        and source_times.shape[0] == eigvecs.shape[0]
    )
    return (fast if fits else general)(eigvecs, perambulator, momenta, source_times)


def solution(mesh):
    placed = (P("snk", ("src", "slab"), None), P("snk", "src", None, None, None), P(), P("src"))

    return jax.shard_map(
        local,
        mesh=mesh,
        in_specs=placed,
        out_specs=P(None, "snk", "src", None, "slab", None),
        check_vma=False,
    )
```

```python
import functools
import math

import jax
import jax.numpy as jnp
from jax import lax
from jax.experimental import pallas as pl
from jax.experimental.pallas import tpu as pltpu
from jax.sharding import PartitionSpec as P


LX = 32
LY = 32
TAIL = 16
CHUNK = 256
F32 = jnp.float32
BF16 = jnp.bfloat16
VMEM = pl.BlockSpec(memory_space=pltpu.VMEM)
SMEM = pl.BlockSpec(memory_space=pltpu.SMEM)


def angles(momenta, xs, ys, zs, lz):
    fx = (momenta[:, 0:1] * xs[None, :] % LX).astype(F32) / LX
    fy = (momenta[:, 1:2] * ys[None, :] % LY).astype(F32) / LY
    fz = (momenta[:, 2:3] * zs[None, :] % lz).astype(F32) / lz
    return 2.0 * math.pi * (fx + fy + fz)


def general(eigvecs, perambulator, momenta, source_times):
    nev = eigvecs.shape[2] // 2
    count = eigvecs.shape[1]
    zpl = count // (LX * LY)
    slabs = lax.axis_size("slab")
    lz = zpl * lax.axis_size("src") * slabs
    sites = jnp.arange(count, dtype=jnp.int32)
    xs = sites % LX
    ys = sites // LX % LY
    zs = sites // (LX * LY) + lax.axis_index(("src", "slab")) * zpl
    angle = angles(momenta, xs, ys, zs, lz)
    vreal = eigvecs[:, :, :nev].astype(F32)
    vimag = eigvecs[:, :, nev:].astype(F32)
    partials = []
    for m in range(angle.shape[0]):
        cosine = jnp.cos(angle[m])[None, :, None]
        sine = jnp.sin(angle[m])[None, :, None]
        phased = jnp.concatenate(
            [cosine * vreal + sine * vimag, cosine * vimag - sine * vreal], axis=2
        ).astype(BF16)
        gram = jnp.einsum("tsa,tsb->tab", eigvecs, phased, preferred_element_type=F32)
        real = gram[:, :nev, :nev] + gram[:, nev:, nev:]
        imag = gram[:, :nev, nev:] - gram[:, nev:, :nev]
        partials.append(jnp.concatenate([real, imag], axis=2))
    partial_value = jnp.stack(partials, axis=1)
    tdev = partial_value.shape[0]
    rows = nev // slabs
    local_times = lax.axis_index("snk") * tdev + jnp.arange(tdev, dtype=jnp.int32)
    slab_part = lax.psum_scatter(partial_value, "slab", scatter_dimension=2, tiled=True)
    share = lax.psum_scatter(slab_part, "src", scatter_dimension=2, tiled=True).astype(BF16)
    sink = lax.all_gather(share, "src", axis=2, tiled=True)
    selector = (source_times[:, None] == local_times[None, :]).astype(BF16)
    term = jnp.dot(selector, sink.reshape(tdev, -1), preferred_element_type=F32)
    picked = lax.psum(term.astype(BF16), "snk")
    picked = picked.reshape((source_times.shape[0],) + sink.shape[1:])
    source = lax.all_gather(picked, "slab", axis=2, tiled=True)
    stacked = jnp.concatenate([sink[..., :nev], sink[..., nev:]], axis=2)
    prod = jnp.einsum("tmra,tsqab->mtsqrb", stacked, perambulator, preferred_element_type=F32)
    creal = prod[..., :rows, :nev] - prod[..., rows:, nev:]
    cimag = prod[..., :rows, nev:] + prod[..., rows:, :nev]
    half = jnp.concatenate([creal, cimag], axis=4).astype(BF16)
    both = jnp.concatenate([source[..., :nev], source[..., nev:]], axis=2)
    quad = jnp.einsum("mtsqrb,smcb->mtsqrc", half, both, preferred_element_type=F32)
    dreal = quad[..., :rows, :nev] + quad[..., rows:, nev:]
    dimag = quad[..., rows:, :nev] - quad[..., :rows, nev:]
    return jnp.concatenate([dreal, dimag], axis=-1)


def turned(x, nev):
    return jnp.concatenate([x[:, nev:], -x[:, :nev]], axis=1)


def circle(f):
    turns = jnp.floor(4.0 * f + 0.5)
    r = (f - 0.25 * turns) * (2.0 * math.pi)
    n = turns.astype(jnp.int32) & 3
    x = r * r
    c = 1.0 + x * (-1 / 2 + x * (1 / 24 + x * (-1 / 720 + x * (1 / 40320))))
    s = r * (1.0 + x * (-1 / 6 + x * (1 / 120 + x * (-1 / 5040 + x * (1 / 362880)))))
    odd = (n & 1) == 1
    cosine = jnp.where(odd, s, c)
    sine = jnp.where(odd, c, s)
    return (
        jnp.where((n == 1) | (n == 2), -cosine, cosine),
        jnp.where(n >= 2, -sine, sine),
    )


def phase(tab, i, y, core, width):
    cy = jnp.broadcast_to(tab[2 + 2 * core, i, pl.ds(y, 1), :], (LX, 128))
    sy = jnp.broadcast_to(tab[3 + 2 * core, i, pl.ds(y, 1), :], (LX, 128))
    cx, sx = tab[0, i], tab[1, i]
    c = cx * cy - sx * sy
    s = sx * cy + cx * sy
    return [jnp.concatenate([x] * (width // 128), axis=1) for x in (c, s)]


def site_sums(pieces, vec, tab, core, wide, tran, sums):
    count, width = vec.shape
    nev = width // 2
    chunk = min(count, CHUNK)

    def spread(c):
        for y in range(c * chunk // LX, (c + 1) * chunk // LX):
            at = pl.ds(y * LX, LX)
            v = vec[at, :].astype(F32)
            u = turned(v, nev)
            for i, k in enumerate(pieces):
                c_, s_ = phase(tab, k, y, core, width)
                wide[at, i * width : (i + 1) * width] = (c_ * v + s_ * u).astype(BF16)

    tran[...] = vec[...].T
    spread(0)
    for c in range(count // chunk):
        at = slice(c * chunk, (c + 1) * chunk)
        for i in range(len(pieces)):
            g = jnp.dot(
                tran[:, at], wide[at, i * width : (i + 1) * width], preferred_element_type=F32
            )
            sums[i] = g if c == 0 else sums[i] + g
        if (c + 1) * chunk < count:
            spread(c + 1)


def own_kernel(nsrc, slabs, lz, pieces, mom_hbm, eig_hbm, acc_ref, tab, vec, *refs):
    mom_ref, wide, tran, sums, mom_sem, sem = refs
    nev = vec.shape[1] // 2
    slab = lax.axis_index("slab")
    src = lax.axis_index("src")
    small = pltpu.make_async_copy(mom_hbm, mom_ref, mom_sem)
    small.start()
    copy = pltpu.make_async_copy(eig_hbm.at[slab], vec, sem)
    copy.start()
    small.wait()
    index = lax.broadcasted_iota(jnp.int32, (LX, 128), 0)
    for k in range(nsrc):
        mom = mom_ref[pl.ds(src ^ k, 1), :]
        px, py, pz = (jnp.broadcast_to(mom[:, i : i + 1], (LX, 128)) for i in range(3))
        tab[0, k], tab[1, k] = circle((px * index % LX).astype(F32) / LX)
        for core in range(2):
            z = src * slabs + (1 - slab if core else slab)
            fz = (pz * z % lz).astype(F32) / lz
            fy = (py * index % LY).astype(F32) / LY
            tab[2 + 2 * core, k], tab[3 + 2 * core, k] = circle(fy + fz)
    copy.wait()
    site_sums(pieces, vec, tab, 0, wide, tran, sums)
    for i in range(len(pieces)):
        acc_ref[i] = sums[i, :nev] + turned(sums[i, nev:], nev)


def sibling_kernel(pieces, times_hbm, eig_ref, tab, acc_ref, *refs):
    outs = refs[: len(pieces)]
    times_ref, wide, tran, sums, sem = refs[len(pieces) :]
    copy = pltpu.make_async_copy(times_hbm, times_ref, sem)
    copy.start()
    width = eig_ref.shape[2]
    nev = width // 2
    site_sums(pieces, eig_ref.at[lax.axis_index("slab")], tab, 1, wide, tran, sums)
    copy.wait()
    for i in range(len(pieces)):
        e = sums[i, :nev] + turned(sums[i, nev:], nev)
        outs[i][:nev, :] = (e + acc_ref[i]).astype(BF16)
        for s in range(times_ref.shape[1]):
            time = jnp.broadcast_to(times_ref[:, s : s + 1].astype(F32), (TAIL, width))
            outs[i][nev + s * TAIL : nev + (s + 1) * TAIL, :] = time.astype(BF16)


def last_kernel(eig_hbm, eig_ref, tab, out, vec, wide, tran, sums, sem):
    nev = vec.shape[1] // 2
    slab = lax.axis_index("slab")
    copy = pltpu.make_async_copy(eig_hbm.at[slab], vec, sem)
    copy.start()
    site_sums([0], eig_ref.at[slab], tab, 1, wide, tran, sums)
    out[...] = sums[0, :nev] + turned(sums[0, nev:], nev)
    copy.wait()
    site_sums([0], vec, tab, 0, wide, tran, sums)
    out[...] = out[...] + (sums[0, :nev] + turned(sums[0, nev:], nev))


def sum_kernel(own, *refs):
    keep, send = refs[-2:]
    rows = keep.shape[0]
    slab = lax.axis_index("slab")
    for out, part in ((keep, slab), (send, 1 - slab)):
        at = pl.multiple_of(part * rows, rows)
        total = own[pl.ds(at, rows), :]
        for r in refs[:-2]:
            total = total + r[pl.ds(at, rows), :].astype(F32)
        out[...] = total.astype(BF16)


def join_kernel(keep, came, out):
    slab = lax.axis_index("slab")
    out[slab] = keep[...]
    out[1 - slab] = came[...]


def pick_kernel(nsnk, nsrc, times_ref, *refs):
    sent = refs[: nsrc - 1]
    seen = refs[nsrc - 1 : nsrc - 1 + nsnk]
    outs = refs[nsrc - 1 + nsnk :]
    tdev, rows, width = seen[0].shape
    nev = width // 2
    snk = lax.axis_index("snk")
    for k in range(nsrc):
        for s in range(outs[k].shape[0]):
            if k == 0:
                want = jnp.full((TAIL, 128), times_ref[s].astype(F32), F32)
            else:
                want = sent[k - 1][nev + s * TAIL : nev + (s + 1) * TAIL, :128].astype(F32)
            mask = []
            for d in range(nsnk):
                for t in range(tdev):
                    time = ((snk ^ d) * tdev + t).astype(F32)
                    one = (want == time).astype(F32).astype(BF16)
                    mask.append(jnp.concatenate([one] * (width // 128), axis=1))
            for r in range(rows // TAIL):
                total = None
                for d in range(nsnk):
                    for t in range(tdev):
                        term = mask[d * tdev + t] * seen[d][t, r * TAIL : (r + 1) * TAIL, :]
                        total = term if total is None else total + term
                outs[k][s, r * TAIL : (r + 1) * TAIL, :] = total


def half_kernel(nsrc, *refs):
    sinks = refs[:nsrc]
    per_ref, out_ref, lhs, rhs = refs[nsrc:]
    tdev, rows, width = sinks[0].shape
    nev = width // 2
    sdev, nq = per_ref.shape[1:3]
    for t in range(tdev):
        for k in range(nsrc):
            lhs[t, k * rows : (k + 1) * rows, :] = sinks[k][t]
        for s in range(sdev):
            for q in range(nq):
                p = per_ref[t, s, q]
                rhs[s, :nev, q * width : (q + 1) * width] = p
                rhs[s, nev:, q * width : (q + 1) * width] = (-turned(p.astype(F32), nev)).astype(BF16)
            h = jnp.dot(lhs[t], rhs[s], preferred_element_type=F32).astype(BF16)
            for q in range(nq):
                for k in range(nsrc):
                    part = h[k * rows : (k + 1) * rows, q * width : (q + 1) * width]
                    out_ref[k, s, t * nq + q] = part


def block_kernel(first, pieces, chained, half_ref, *refs):
    mine = refs[:pieces]
    other = refs[pieces : 2 * pieces]
    out_hbm, rhs, buf, sem = refs[2 * pieces + chained :]
    sdev, rows, width = mine[0].shape
    nev = width // 2
    slots, tdev, nq = buf.shape[:3]
    slab = lax.axis_index("slab")
    src = lax.axis_index("src")
    copies = []
    for j in range(pieces):
        for s in range(sdev):
            n = len(copies)
            slot, part = n % slots, n % 2
            lower = jnp.where(slab == 0, mine[j][s], other[j][s])
            upper = jnp.where(slab == 0, other[j][s], mine[j][s])
            for at, x in ((0, lower), (rows, upper)):
                rhs[part, at : at + rows, :] = x
                rhs[part, nev + at : nev + at + rows, :] = (-turned(x.astype(F32), nev)).astype(BF16)
            if n >= slots:
                for copy in copies[n - slots]:
                    copy.wait()
            out = lax.dot_general(
                half_ref[first + j, s].reshape(tdev * nq * rows, width),
                rhs[part],
                (((1,), (1,)), ((), ())),
                preferred_element_type=F32,
            )
            buf[slot] = out.reshape(tdev, nq, rows, width)
            copies.append(
                [
                    pltpu.make_async_copy(
                        buf.at[slot, t], out_hbm.at[src ^ (first + j), t, s], sem.at[slot, t]
                    )
                    for t in range(tdev)
                ]
            )
            for copy in copies[n]:
                copy.start()
    for group in copies[-slots:]:
        for copy in group:
            copy.wait()


def fast(eigvecs, perambulator, momenta, source_times):
    nsrc, nsnk, slabs = (lax.axis_size(a) for a in ("src", "snk", "slab"))
    tdev, count, width = eigvecs.shape
    sdev = source_times.shape[0]
    nq = perambulator.shape[2]
    nev = width // 2
    rows = nev // slabs
    lz = count // (LX * LY) * nsrc * slabs

    def shape(dims, dtype=BF16):
        return jax.ShapeDtypeStruct(dims, dtype)

    def params(mib):
        return pltpu.CompilerParams(vmem_limit_bytes=mib * 2**20)

    def cost(flops, moved):
        return pl.CostEstimate(flops=flops, bytes_accessed=moved, transcendentals=0)

    def swap(x):
        return lax.ppermute(x, "slab", [(0, 1), (1, 0)])

    def cross(x, k):
        return lax.ppermute(x, "src", [(i, i ^ k) for i in range(nsrc)])

    def along(x, d):
        return lax.ppermute(x, "snk", [(i, i ^ d) for i in range(nsnk)])

    theirs = swap(eigvecs)
    work = 2 * width * count * width
    hbm = pl.BlockSpec(memory_space=pltpu.HBM)
    sent = list(range(nsrc - 1, 0, -1))

    def grams(n):
        return [
            pltpu.VMEM((count, n * width), BF16),
            pltpu.VMEM((width, count), BF16),
            pltpu.VMEM((n, width, width), F32),
        ]

    vec = pltpu.VMEM((count, width), BF16)
    sem = pltpu.SemaphoreType.DMA

    def held(x):
        return pltpu.with_memory_space_constraint(x, pltpu.HBM)

    eigs = held(eigvecs)
    acc, tab = pl.pallas_call(
        functools.partial(own_kernel, nsrc, slabs, lz, sent),
        out_shape=[shape((len(sent), nev, width), F32), shape((6, nsrc, LX, 128), F32)],
        in_specs=[hbm, hbm],
        out_specs=[VMEM] * 2,
        scratch_shapes=[vec, pltpu.VMEM(momenta.shape, jnp.int32)] + grams(len(sent)) + [sem] * 2,
        cost_estimate=cost(len(sent) * work, 2 * count * width),
        compiler_params=params(12),
        name="gram_own",
    )(held(momenta), eigs)
    parts = pl.pallas_call(
        functools.partial(sibling_kernel, sent),
        out_shape=[shape((nev + sdev * TAIL, width))] * len(sent),
        in_specs=[hbm] + [VMEM] * 3,
        out_specs=[VMEM] * len(sent),
        scratch_shapes=[pltpu.VMEM((1, sdev), jnp.int32)] + grams(len(sent)) + [sem],
        cost_estimate=cost(len(sent) * work, 2 * count * width),
        compiler_params=params(12),
        name="gram_sibling",
    )(held(source_times.reshape(1, sdev)), theirs, tab, acc)
    got = [cross(part, k) for k, part in zip(sent, parts)][::-1]
    own = pl.pallas_call(
        last_kernel,
        out_shape=shape((nev, width), F32),
        in_specs=[hbm, VMEM, VMEM],
        out_specs=VMEM,
        scratch_shapes=[vec] + grams(1) + [sem],
        cost_estimate=cost(2 * work, 2 * count * width),
        compiler_params=params(12),
        name="gram_last",
    )(eigs, theirs, tab)
    keep, send = pl.pallas_call(
        sum_kernel,
        out_shape=[shape((rows, width))] * 2,
        in_specs=[VMEM] * nsrc,
        out_specs=[VMEM] * 2,
        compiler_params=params(4),
        name="sum",
    )(own, *got)
    red = pl.pallas_call(
        join_kernel,
        out_shape=shape((tdev, rows, width)),
        in_specs=[VMEM] * 2,
        out_specs=VMEM,
        compiler_params=params(4),
        name="join",
    )(keep, swap(send))
    seen = [red] + [along(red, d) for d in range(1, nsnk)]
    sinks = [red] + [cross(red, k) for k in range(1, nsrc)]
    picked = pl.pallas_call(
        functools.partial(pick_kernel, nsnk, nsrc),
        out_shape=[shape((sdev, rows, width))] * nsrc,
        in_specs=[SMEM] + [VMEM] * (nsrc - 1 + nsnk),
        out_specs=[VMEM] * nsrc,
        compiler_params=params(8),
        name="pick",
    )(source_times, *got, *seen)

    tq = tdev * nq
    half = pl.pallas_call(
        functools.partial(half_kernel, nsrc),
        out_shape=shape((nsrc, sdev, tq, rows, width)),
        in_specs=[VMEM] * (nsrc + 1),
        out_specs=VMEM,
        scratch_shapes=[
            pltpu.VMEM((tdev, nsrc * rows, width), BF16),
            pltpu.VMEM((sdev, width, nq * width), BF16),
        ],
        cost_estimate=cost(2 * tq * sdev * nsrc * rows * width * width, 2 * perambulator.size),
        compiler_params=params(16),
        name="half",
    )(*sinks, perambulator)

    mine = [picked[0]] + [cross(picked[k], k) for k in range(1, nsrc)]
    other = [swap(x) for x in mine]

    def finish(first, n, before):
        chained = before is not None
        slots = min(n * sdev, 4)
        return pl.pallas_call(
            functools.partial(block_kernel, first, n, chained),
            out_shape=shape((nsrc, tdev, sdev, nq, rows, width), F32),
            in_specs=[VMEM] * (1 + 2 * n) + [hbm] * chained,
            out_specs=hbm,
            scratch_shapes=[
                pltpu.VMEM((2, width, width), BF16),
                pltpu.VMEM((slots, tdev, nq, rows, width), F32),
                pltpu.SemaphoreType.DMA((slots, tdev)),
            ],
            input_output_aliases={1 + 2 * n: 0} if chained else {},
            cost_estimate=cost(
                2 * n * tq * sdev * rows * width * width, 4 * n * tq * sdev * rows * width
            ),
            compiler_params=params(16),
        )(half, *mine[first : first + n], *other[first : first + n], *([before] if chained else []))

    blocks = finish(0, 1, None)
    return finish(1, nsrc - 1, blocks)


def local(eigvecs, perambulator, momenta, source_times):
    nsrc = lax.axis_size("src")
    fits = (
        lax.axis_size("slab") == 2
        and momenta.shape[0] == nsrc
        and nsrc & (nsrc - 1) == 0
        and eigvecs.shape[1] == LX * LY
        and source_times.shape[0] == eigvecs.shape[0]
    )
    return (fast if fits else general)(eigvecs, perambulator, momenta, source_times)


def solution(mesh):
    placed = (P("snk", ("src", "slab"), None), P("snk", "src", None, None, None), P(), P("src"))

    return jax.shard_map(
        local,
        mesh=mesh,
        in_specs=placed,
        out_specs=P(None, "snk", "src", None, "slab", None),
        check_vma=False,
    )
```

```python
import functools
import math

import jax
import jax.numpy as jnp
from jax import lax
from jax.experimental import pallas as pl
from jax.experimental.pallas import tpu as pltpu
from jax.sharding import PartitionSpec as P


LX = 32
LY = 32
TAIL = 16
CHUNK = 256
F32 = jnp.float32
BF16 = jnp.bfloat16
VMEM = pl.BlockSpec(memory_space=pltpu.VMEM)
SMEM = pl.BlockSpec(memory_space=pltpu.SMEM)


def angles(momenta, xs, ys, zs, lz):
    fx = (momenta[:, 0:1] * xs[None, :] % LX).astype(F32) / LX
    fy = (momenta[:, 1:2] * ys[None, :] % LY).astype(F32) / LY
    fz = (momenta[:, 2:3] * zs[None, :] % lz).astype(F32) / lz
    return 2.0 * math.pi * (fx + fy + fz)


def general(eigvecs, perambulator, momenta, source_times):
    nev = eigvecs.shape[2] // 2
    count = eigvecs.shape[1]
    zpl = count // (LX * LY)
    slabs = lax.axis_size("slab")
    lz = zpl * lax.axis_size("src") * slabs
    sites = jnp.arange(count, dtype=jnp.int32)
    xs = sites % LX
    ys = sites // LX % LY
    zs = sites // (LX * LY) + lax.axis_index(("src", "slab")) * zpl
    angle = angles(momenta, xs, ys, zs, lz)
    vreal = eigvecs[:, :, :nev].astype(F32)
    vimag = eigvecs[:, :, nev:].astype(F32)
    partials = []
    for m in range(angle.shape[0]):
        cosine = jnp.cos(angle[m])[None, :, None]
        sine = jnp.sin(angle[m])[None, :, None]
        phased = jnp.concatenate(
            [cosine * vreal + sine * vimag, cosine * vimag - sine * vreal], axis=2
        ).astype(BF16)
        gram = jnp.einsum("tsa,tsb->tab", eigvecs, phased, preferred_element_type=F32)
        real = gram[:, :nev, :nev] + gram[:, nev:, nev:]
        imag = gram[:, :nev, nev:] - gram[:, nev:, :nev]
        partials.append(jnp.concatenate([real, imag], axis=2))
    partial_value = jnp.stack(partials, axis=1)
    tdev = partial_value.shape[0]
    rows = nev // slabs
    local_times = lax.axis_index("snk") * tdev + jnp.arange(tdev, dtype=jnp.int32)
    slab_part = lax.psum_scatter(partial_value, "slab", scatter_dimension=2, tiled=True)
    share = lax.psum_scatter(slab_part, "src", scatter_dimension=2, tiled=True).astype(BF16)
    sink = lax.all_gather(share, "src", axis=2, tiled=True)
    selector = (source_times[:, None] == local_times[None, :]).astype(BF16)
    term = jnp.dot(selector, sink.reshape(tdev, -1), preferred_element_type=F32)
    picked = lax.psum(term.astype(BF16), "snk")
    picked = picked.reshape((source_times.shape[0],) + sink.shape[1:])
    source = lax.all_gather(picked, "slab", axis=2, tiled=True)
    stacked = jnp.concatenate([sink[..., :nev], sink[..., nev:]], axis=2)
    prod = jnp.einsum("tmra,tsqab->mtsqrb", stacked, perambulator, preferred_element_type=F32)
    creal = prod[..., :rows, :nev] - prod[..., rows:, nev:]
    cimag = prod[..., :rows, nev:] + prod[..., rows:, :nev]
    half = jnp.concatenate([creal, cimag], axis=4).astype(BF16)
    both = jnp.concatenate([source[..., :nev], source[..., nev:]], axis=2)
    quad = jnp.einsum("mtsqrb,smcb->mtsqrc", half, both, preferred_element_type=F32)
    dreal = quad[..., :rows, :nev] + quad[..., rows:, nev:]
    dimag = quad[..., rows:, :nev] - quad[..., :rows, nev:]
    return jnp.concatenate([dreal, dimag], axis=-1)


def turned(x, nev):
    return jnp.concatenate([x[:, nev:], -x[:, :nev]], axis=1)


def circle(f):
    turns = jnp.floor(4.0 * f + 0.5)
    r = (f - 0.25 * turns) * (2.0 * math.pi)
    n = turns.astype(jnp.int32) & 3
    x = r * r
    c = 1.0 + x * (-1 / 2 + x * (1 / 24 + x * (-1 / 720 + x * (1 / 40320))))
    s = r * (1.0 + x * (-1 / 6 + x * (1 / 120 + x * (-1 / 5040 + x * (1 / 362880)))))
    odd = (n & 1) == 1
    cosine = jnp.where(odd, s, c)
    sine = jnp.where(odd, c, s)
    return (
        jnp.where((n == 1) | (n == 2), -cosine, cosine),
        jnp.where(n >= 2, -sine, sine),
    )


def phase(tab, i, y, core, width):
    cy = jnp.broadcast_to(tab[2 + 2 * core, i, pl.ds(y, 1), :], (LX, 128))
    sy = jnp.broadcast_to(tab[3 + 2 * core, i, pl.ds(y, 1), :], (LX, 128))
    cx, sx = tab[0, i], tab[1, i]
    c = cx * cy - sx * sy
    s = sx * cy + cx * sy
    return [jnp.concatenate([x] * (width // 128), axis=1) for x in (c, s)]


def site_sums(pieces, vec, tab, core, wide, lhs, sums):
    count, width = vec.shape
    nev = width // 2
    chunk = min(count, CHUNK)

    def spread(c):
        for y in range(c * chunk // LX, (c + 1) * chunk // LX):
            at = pl.ds(y * LX, LX)
            v = vec[at, :].astype(F32)
            u = turned(v, nev)
            for i, k in enumerate(pieces):
                c_, s_ = phase(tab, k, y, core, width)
                wide[at, i * width : (i + 1) * width] = (c_ * v + s_ * u).astype(BF16)

    spread(0)
    for c in range(count // chunk):
        at = slice(c * chunk, (c + 1) * chunk)
        for i in range(len(pieces)):
            g = jnp.dot(
                lhs[:, at], wide[at, i * width : (i + 1) * width], preferred_element_type=F32
            )
            sums[i] = g if c == 0 else sums[i] + g
        if (c + 1) * chunk < count:
            spread(c + 1)


def own_kernel(nsrc, slabs, lz, pieces, mom_hbm, eig_hbm, acc_ref, tab, vec, *refs):
    mom_ref, wide, tran, sums, mom_sem, sem = refs
    nev = vec.shape[1] // 2
    slab = lax.axis_index("slab")
    src = lax.axis_index("src")
    small = pltpu.make_async_copy(mom_hbm, mom_ref, mom_sem)
    small.start()
    copy = pltpu.make_async_copy(eig_hbm.at[slab], vec, sem)
    copy.start()
    small.wait()
    index = lax.broadcasted_iota(jnp.int32, (LX, 128), 0)
    for k in range(nsrc):
        mom = mom_ref[pl.ds(src ^ k, 1), :]
        px, py, pz = (jnp.broadcast_to(mom[:, i : i + 1], (LX, 128)) for i in range(3))
        tab[0, k], tab[1, k] = circle((px * index % LX).astype(F32) / LX)
        for core in range(2):
            z = src * slabs + (1 - slab if core else slab)
            fz = (pz * z % lz).astype(F32) / lz
            fy = (py * index % LY).astype(F32) / LY
            tab[2 + 2 * core, k], tab[3 + 2 * core, k] = circle(fy + fz)
    copy.wait()
    tran[...] = vec[...].T
    site_sums(pieces, vec, tab, 0, wide, tran, sums)
    for i in range(len(pieces)):
        acc_ref[i] = sums[i, :nev] + turned(sums[i, nev:], nev)


def same_kernel(pieces, times_hbm, eig_ref, tab, acc_ref, *refs):
    n = len(pieces)
    same = refs[:n]
    wide, rest, times_ref, tran, lhs, sums, sem = refs[n:]
    copy = pltpu.make_async_copy(times_hbm, times_ref, sem)
    copy.start()
    width = eig_ref.shape[2]
    nev = width // 2
    rows = nev // 2
    slab = lax.axis_index("slab")
    vec = eig_ref.at[slab]
    tran[...] = vec[...].T
    for i in range(2):
        lower = tran[i * nev : i * nev + rows, :]
        upper = tran[i * nev + rows : (i + 1) * nev, :]
        lhs[i * rows : (i + 1) * rows, :] = jnp.where(slab == 0, lower, upper)
        rest[i * rows : (i + 1) * rows, :] = jnp.where(slab == 0, upper, lower)
    site_sums(pieces, vec, tab, 1, wide, lhs, sums)
    copy.wait()
    for i, k in enumerate(pieces):
        e = sums[i, :rows] + turned(sums[i, rows:], nev)
        e = e + jnp.where(slab == 0, acc_ref[i, :rows], acc_ref[i, rows:])
        same[i][:rows, :] = e.astype(same[i].dtype)
        if k:
            for s in range(times_ref.shape[1]):
                time = jnp.broadcast_to(times_ref[:, s : s + 1].astype(F32), (TAIL, width))
                same[i][rows + s * TAIL : rows + (s + 1) * TAIL, :] = time.astype(BF16)


def cross_kernel(wide, rest, acc_ref, *outs):
    rows, width = outs[0].shape
    nev = width // 2
    slab = lax.axis_index("slab")
    for i, out in enumerate(outs):
        g = jnp.dot(rest[...], wide[:, i * width : (i + 1) * width], preferred_element_type=F32)
        e = g[:rows] + turned(g[rows:], nev)
        e = e + jnp.where(slab == 0, acc_ref[i, rows:], acc_ref[i, :rows])
        out[...] = e.astype(out.dtype)


def sum_kernel(own, *refs):
    out = refs[-1]
    rows = out.shape[0]
    total = own[...]
    for r in refs[:-1]:
        total = total + r[:rows, :].astype(F32)
    out[...] = total.astype(BF16)


def both_kernel(own, *refs):
    done = refs[-3]
    out, both = refs[-2:]
    total = own[...]
    for r in refs[:-3]:
        total = total + r[...].astype(F32)
    red = total.astype(BF16)
    out[...] = red
    slab = lax.axis_index("slab")
    both[0] = jnp.where(slab == 0, done[...], red)
    both[1] = jnp.where(slab == 0, red, done[...])


def pick_kernel(nsrc, labels, chained, times_ref, *refs):
    n = len(labels)
    sent = refs[: nsrc - 1]
    seen = refs[nsrc - 1 : nsrc - 1 + n]
    before = refs[nsrc - 1 + n : -nsrc]
    outs = refs[-nsrc:]
    rows, width = seen[0].shape[-2:]
    snk = lax.axis_index("snk")
    slab = lax.axis_index("slab")
    for k in range(nsrc):
        for s in range(outs[k].shape[0]):
            if k == 0:
                want = jnp.full((TAIL, 128), times_ref[s].astype(F32), F32)
            else:
                want = sent[k - 1][rows + s * TAIL : rows + (s + 1) * TAIL, :128].astype(F32)
            mask = []
            for d, other in labels:
                parts = (0, 1) if other is None else (1 - slab if other else slab,)
                for part in parts:
                    time = ((snk ^ d) * 2 + part).astype(F32)
                    one = (want == time).astype(F32).astype(BF16)
                    mask.append(jnp.concatenate([one] * (width // 128), axis=1))
            for r in range(rows // TAIL):
                at = slice(r * TAIL, (r + 1) * TAIL)
                total = before[k][s, at, :] if chained else None
                views = []
                for (_, other), x in zip(labels, seen):
                    views += [x[at, :]] if other is not None else [x[0, at, :], x[1, at, :]]
                for one, x in zip(mask, views):
                    term = one * x
                    total = term if total is None else total + term
                outs[k][s, at, :] = total


def half_kernel(pieces, *refs):
    sinks = refs[:pieces]
    per_ref = refs[pieces]
    outs = refs[pieces + 1 : 2 * pieces + 1]
    lhs, rhs = refs[2 * pieces + 1 :]
    tdev, rows, width = sinks[0].shape
    nev = width // 2
    sdev, nq = per_ref.shape[1:3]
    for t in range(tdev):
        for k in range(pieces):
            lhs[t, k * rows : (k + 1) * rows, :] = sinks[k][t]
        for s in range(sdev):
            for q in range(nq):
                p = per_ref[t, s, q]
                rhs[s, :nev, q * width : (q + 1) * width] = p
                rhs[s, nev:, q * width : (q + 1) * width] = (-turned(p.astype(F32), nev)).astype(BF16)
            h = jnp.dot(lhs[t], rhs[s], preferred_element_type=F32).astype(BF16)
            for q in range(nq):
                for k in range(pieces):
                    part = h[k * rows : (k + 1) * rows, q * width : (q + 1) * width]
                    outs[k][s, t * nq + q] = part


def block_kernel(pieces, chained, *refs):
    n = len(pieces)
    half, mine, other = refs[:n], refs[n : 2 * n], refs[2 * n : 3 * n]
    out_hbm, rhs, buf, sem = refs[3 * n + chained :]
    sdev, rows, width = mine[0].shape
    nev = width // 2
    tdev, nq = buf.shape[1:3]
    slab = lax.axis_index("slab")
    src = lax.axis_index("src")
    copies = []
    for j, k in enumerate(pieces):
        for s in range(sdev):
            slot, part = j * sdev + s, s % 2
            lower = jnp.where(slab == 0, mine[j][s], other[j][s])
            upper = jnp.where(slab == 0, other[j][s], mine[j][s])
            for at, x in ((0, lower), (rows, upper)):
                rhs[part, at : at + rows, :] = x
                rhs[part, nev + at : nev + at + rows, :] = (-turned(x.astype(F32), nev)).astype(BF16)
            out = lax.dot_general(
                half[j][s].reshape(tdev * nq * rows, width),
                rhs[part],
                (((1,), (1,)), ((), ())),
                preferred_element_type=F32,
            )
            buf[slot] = out.reshape(tdev, nq, rows, width)
            for t in range(tdev):
                copies.append(
                    pltpu.make_async_copy(
                        buf.at[slot, t], out_hbm.at[src ^ k, t, s], sem.at[slot, t]
                    )
                )
                copies[-1].start()
    for copy in copies:
        copy.wait()


def fast(eigvecs, perambulator, momenta, source_times):
    nsrc, nsnk, slabs = (lax.axis_size(a) for a in ("src", "snk", "slab"))
    tdev, count, width = eigvecs.shape
    sdev = source_times.shape[0]
    nq = perambulator.shape[2]
    nev = width // 2
    rows = nev // slabs
    lz = count // (LX * LY) * nsrc * slabs

    def shape(dims, dtype=BF16):
        return jax.ShapeDtypeStruct(dims, dtype)

    def params(mib):
        return pltpu.CompilerParams(vmem_limit_bytes=mib * 2**20)

    def cost(flops, moved):
        return pl.CostEstimate(flops=flops, bytes_accessed=moved, transcendentals=0)

    def swap(x):
        return lax.ppermute(x, "slab", [(0, 1), (1, 0)])

    def cross(x, k):
        return lax.ppermute(x, "src", [(i, i ^ k) for i in range(nsrc)])

    def far(x, k):
        pairs = [(2 * i + j, 2 * (i ^ k) + 1 - j) for i in range(nsrc) for j in range(2)]
        return lax.ppermute(x, ("src", "slab"), pairs)

    def along(x, d):
        return lax.ppermute(x, "snk", [(i, i ^ d) for i in range(nsnk)])

    theirs = swap(eigvecs)
    work = 2 * width * count * width
    hbm = pl.BlockSpec(memory_space=pltpu.HBM)
    sent = list(range(nsrc - 1, -1, -1))

    def grams(n):
        return [
            pltpu.VMEM((count, n * width), BF16),
            pltpu.VMEM((width, count), BF16),
            pltpu.VMEM((n, width, width), F32),
        ]

    vec = pltpu.VMEM((count, width), BF16)
    sem = pltpu.SemaphoreType.DMA

    def held(x):
        return pltpu.with_memory_space_constraint(x, pltpu.HBM)

    eigs = held(eigvecs)
    acc, tab = pl.pallas_call(
        functools.partial(own_kernel, nsrc, slabs, lz, sent),
        out_shape=[shape((len(sent), nev, width), F32), shape((6, nsrc, LX, 128), F32)],
        in_specs=[hbm, hbm],
        out_specs=[VMEM] * 2,
        scratch_shapes=[vec, pltpu.VMEM(momenta.shape, jnp.int32)] + grams(len(sent)) + [sem] * 2,
        cost_estimate=cost(len(sent) * work, 2 * count * width),
        compiler_params=params(12),
        name="gram_own",
    )(held(momenta), eigs)
    parts = pl.pallas_call(
        functools.partial(same_kernel, sent),
        out_shape=[shape((rows + sdev * TAIL, width)) if k else shape((rows, width), F32) for k in sent]
        + [shape((count, nsrc * width)), shape((2 * rows, count))],
        in_specs=[hbm] + [VMEM] * 3,
        out_specs=[VMEM] * (nsrc + 2),
        scratch_shapes=[
            pltpu.VMEM((1, sdev), jnp.int32),
            pltpu.VMEM((width, count), BF16),
            pltpu.VMEM((2 * rows, count), BF16),
            pltpu.VMEM((nsrc, 2 * rows, width), F32),
            sem,
        ],
        cost_estimate=cost(nsrc * work // 2, 2 * count * width),
        compiler_params=params(12),
        name="gram_same",
    )(held(source_times.reshape(1, sdev)), theirs, tab, acc)
    same = dict(zip(sent, parts))
    other = pl.pallas_call(
        cross_kernel,
        out_shape=[shape((rows, width), BF16 if k else F32) for k in sent],
        in_specs=[VMEM] * 3,
        out_specs=[VMEM] * nsrc,
        cost_estimate=cost(nsrc * work // 2, 2 * count * width),
        compiler_params=params(6),
        name="gram_cross",
    )(*parts[nsrc:], acc)
    other = dict(zip(sent, other))
    got = [cross(same[k], k) for k in range(1, nsrc)]
    more = [far(other[k], k) for k in range(1, nsrc)]
    red = pl.pallas_call(
        sum_kernel,
        out_shape=shape((rows, width)),
        in_specs=[VMEM] * nsrc,
        out_specs=VMEM,
        compiler_params=params(4),
        name="sum_same",
    )(same[0], *got)
    red_far, both = pl.pallas_call(
        both_kernel,
        out_shape=[shape((rows, width)), shape((tdev, rows, width))],
        in_specs=[VMEM] * (nsrc + 1),
        out_specs=[VMEM] * 2,
        compiler_params=params(4),
        name="sum_both",
    )(swap(other[0]), *more, red)
    views = {0: {0: red, 1: red_far}}
    seen = [((0, p), x) for p, x in views[0].items()]
    for bit in reversed([1 << i for i in range(nsnk.bit_length() - 1)]):
        for d in sorted(views):
            if bit == 1 and d == 0 and nsnk > 2:
                seen.append(((1, None), along(both, 1)))
                continue
            views[d | bit] = {p: along(x, bit) for p, x in views[d].items()}
            seen += [((d | bit, p), x) for p, x in views[d | bit].items()]
    labels, seen = zip(*seen)
    sinks = [both] + [cross(both, k) for k in range(1, nsrc)]

    def pick(which, before):
        return pl.pallas_call(
            functools.partial(pick_kernel, nsrc, [labels[i] for i in which], bool(before)),
            out_shape=[shape((sdev, rows, width))] * nsrc,
            in_specs=[SMEM] + [VMEM] * (nsrc - 1 + len(which) + len(before)),
            out_specs=[VMEM] * nsrc,
            compiler_params=params(8),
        )(source_times, *got, *(seen[i] for i in which), *before)

    late = len(labels) - 1
    picked = pick(list(range(late)), [])
    picked = pick([late], picked)

    tq = tdev * nq

    def halves(which):
        n = len(which)
        out = pl.pallas_call(
            functools.partial(half_kernel, n),
            out_shape=[shape((sdev, tq, rows, width))] * n,
            in_specs=[VMEM] * (n + 1),
            out_specs=[VMEM] * n,
            scratch_shapes=[
                pltpu.VMEM((tdev, n * rows, width), BF16),
                pltpu.VMEM((sdev, width, nq * width), BF16),
            ],
            cost_estimate=cost(2 * tq * sdev * n * rows * width * width, 2 * perambulator.size),
            compiler_params=params(12),
        )(*(sinks[k] for k in which), perambulator)
        return dict(zip(which, out))

    half = halves(list(range(nsrc)))

    mine = [picked[0]] + [cross(picked[k], k) for k in range(1, nsrc)]
    other = [swap(x) for x in mine]

    def finish(which, before):
        n = len(which)
        chained = before is not None
        return pl.pallas_call(
            functools.partial(block_kernel, which, chained),
            out_shape=shape((nsrc, tdev, sdev, nq, rows, width), F32),
            in_specs=[VMEM] * (3 * n) + [hbm] * chained,
            out_specs=hbm,
            scratch_shapes=[
                pltpu.VMEM((2, width, width), BF16),
                pltpu.VMEM((n * sdev, tdev, nq, rows, width), F32),
                pltpu.SemaphoreType.DMA((n * sdev, tdev)),
            ],
            input_output_aliases={3 * n: 0} if chained else {},
            cost_estimate=cost(
                2 * n * tq * sdev * rows * width * width, 4 * n * tq * sdev * rows * width
            ),
            compiler_params=params(16),
        )(
            *(x[k] for x in (half, mine, other) for k in which),
            *([before] if chained else []),
        )

    blocks = finish([0], None)
    return finish(list(range(1, nsrc)), blocks)


def local(eigvecs, perambulator, momenta, source_times):
    nsrc = lax.axis_size("src")
    fits = (
        lax.axis_size("slab") == 2
        and momenta.shape[0] == nsrc
        and nsrc & (nsrc - 1) == 0
        and lax.axis_size("snk") & (lax.axis_size("snk") - 1) == 0
        and eigvecs.shape[0] == 2
        and eigvecs.shape[1] == LX * LY
        and source_times.shape[0] == eigvecs.shape[0]
    )
    return (fast if fits else general)(eigvecs, perambulator, momenta, source_times)


def solution(mesh):
    placed = (P("snk", ("src", "slab"), None), P("snk", "src", None, None, None), P(), P("src"))

    return jax.shard_map(
        local,
        mesh=mesh,
        in_specs=placed,
        out_specs=P(None, "snk", "src", None, "slab", None),
        check_vma=False,
    )
```

```python
import functools
import math

import jax
import jax.numpy as jnp
from jax import lax
from jax.experimental import pallas as pl
from jax.experimental.pallas import tpu as pltpu
from jax.sharding import PartitionSpec as P


LX = 32
LY = 32
TAIL = 16
CHUNK = 256
F32 = jnp.float32
BF16 = jnp.bfloat16
VMEM = pl.BlockSpec(memory_space=pltpu.VMEM)


def angles(momenta, xs, ys, zs, lz):
    fx = (momenta[:, 0:1] * xs[None, :] % LX).astype(F32) / LX
    fy = (momenta[:, 1:2] * ys[None, :] % LY).astype(F32) / LY
    fz = (momenta[:, 2:3] * zs[None, :] % lz).astype(F32) / lz
    return 2.0 * math.pi * (fx + fy + fz)


def general(eigvecs, perambulator, momenta, source_times):
    nev = eigvecs.shape[2] // 2
    count = eigvecs.shape[1]
    zpl = count // (LX * LY)
    slabs = lax.axis_size("slab")
    lz = zpl * lax.axis_size("src") * slabs
    sites = jnp.arange(count, dtype=jnp.int32)
    xs = sites % LX
    ys = sites // LX % LY
    zs = sites // (LX * LY) + lax.axis_index(("src", "slab")) * zpl
    angle = angles(momenta, xs, ys, zs, lz)
    vreal = eigvecs[:, :, :nev].astype(F32)
    vimag = eigvecs[:, :, nev:].astype(F32)
    partials = []
    for m in range(angle.shape[0]):
        cosine = jnp.cos(angle[m])[None, :, None]
        sine = jnp.sin(angle[m])[None, :, None]
        phased = jnp.concatenate(
            [cosine * vreal + sine * vimag, cosine * vimag - sine * vreal], axis=2
        ).astype(BF16)
        gram = jnp.einsum("tsa,tsb->tab", eigvecs, phased, preferred_element_type=F32)
        real = gram[:, :nev, :nev] + gram[:, nev:, nev:]
        imag = gram[:, :nev, nev:] - gram[:, nev:, :nev]
        partials.append(jnp.concatenate([real, imag], axis=2))
    partial_value = jnp.stack(partials, axis=1)
    tdev = partial_value.shape[0]
    rows = nev // slabs
    local_times = lax.axis_index("snk") * tdev + jnp.arange(tdev, dtype=jnp.int32)
    slab_part = lax.psum_scatter(partial_value, "slab", scatter_dimension=2, tiled=True)
    share = lax.psum_scatter(slab_part, "src", scatter_dimension=2, tiled=True).astype(BF16)
    sink = lax.all_gather(share, "src", axis=2, tiled=True)
    selector = (source_times[:, None] == local_times[None, :]).astype(BF16)
    term = jnp.dot(selector, sink.reshape(tdev, -1), preferred_element_type=F32)
    picked = lax.psum(term.astype(BF16), "snk")
    picked = picked.reshape((source_times.shape[0],) + sink.shape[1:])
    source = lax.all_gather(picked, "slab", axis=2, tiled=True)
    stacked = jnp.concatenate([sink[..., :nev], sink[..., nev:]], axis=2)
    prod = jnp.einsum("tmra,tsqab->mtsqrb", stacked, perambulator, preferred_element_type=F32)
    creal = prod[..., :rows, :nev] - prod[..., rows:, nev:]
    cimag = prod[..., :rows, nev:] + prod[..., rows:, :nev]
    half = jnp.concatenate([creal, cimag], axis=4).astype(BF16)
    both = jnp.concatenate([source[..., :nev], source[..., nev:]], axis=2)
    quad = jnp.einsum("mtsqrb,smcb->mtsqrc", half, both, preferred_element_type=F32)
    dreal = quad[..., :rows, :nev] + quad[..., rows:, nev:]
    dimag = quad[..., rows:, :nev] - quad[..., :rows, nev:]
    return jnp.concatenate([dreal, dimag], axis=-1)


def turned(x, nev):
    return jnp.concatenate([x[:, nev:], -x[:, :nev]], axis=1)


def circle(f):
    turns = jnp.floor(4.0 * f + 0.5)
    r = (f - 0.25 * turns) * (2.0 * math.pi)
    n = turns.astype(jnp.int32) & 3
    x = r * r
    c = 1.0 + x * (-1 / 2 + x * (1 / 24 + x * (-1 / 720 + x * (1 / 40320))))
    s = r * (1.0 + x * (-1 / 6 + x * (1 / 120 + x * (-1 / 5040 + x * (1 / 362880)))))
    odd = (n & 1) == 1
    cosine = jnp.where(odd, s, c)
    sine = jnp.where(odd, c, s)
    return (
        jnp.where((n == 1) | (n == 2), -cosine, cosine),
        jnp.where(n >= 2, -sine, sine),
    )


def phase(tab, i, y, core, width):
    cy = jnp.broadcast_to(tab[2 + 2 * core, i, pl.ds(y, 1), :], (LX, 128))
    sy = jnp.broadcast_to(tab[3 + 2 * core, i, pl.ds(y, 1), :], (LX, 128))
    cx, sx = tab[0, i], tab[1, i]
    c = cx * cy - sx * sy
    s = sx * cy + cx * sy
    return [jnp.concatenate([x] * (width // 128), axis=1) for x in (c, s)]


def site_sums(pieces, vec, tab, core, wide, lhs, sums):
    count, width = vec.shape
    nev = width // 2
    chunk = min(count, CHUNK)

    def spread(c):
        for y in range(c * chunk // LX, (c + 1) * chunk // LX):
            at = pl.ds(y * LX, LX)
            v = vec[at, :].astype(F32)
            u = turned(v, nev)
            for i, k in enumerate(pieces):
                c_, s_ = phase(tab, k, y, core, width)
                wide[at, i * width : (i + 1) * width] = (c_ * v + s_ * u).astype(BF16)

    spread(0)
    for c in range(count // chunk):
        at = slice(c * chunk, (c + 1) * chunk)
        for i in range(len(pieces)):
            g = jnp.dot(
                lhs[:, at], wide[at, i * width : (i + 1) * width], preferred_element_type=F32
            )
            sums[i] = g if c == 0 else sums[i] + g
        if (c + 1) * chunk < count:
            spread(c + 1)


def own_kernel(nsrc, slabs, lz, pieces, mom_hbm, eig_hbm, acc_ref, tab, vec, *refs):
    mom_ref, wide, tran, sums, mom_sem, sem = refs
    nev = vec.shape[1] // 2
    slab = lax.axis_index("slab")
    src = lax.axis_index("src")
    small = pltpu.make_async_copy(mom_hbm, mom_ref, mom_sem)
    small.start()
    copy = pltpu.make_async_copy(eig_hbm.at[slab], vec, sem)
    copy.start()
    small.wait()
    index = lax.broadcasted_iota(jnp.int32, (LX, 128), 0)
    for k in range(nsrc):
        mom = mom_ref[pl.ds(src ^ k, 1), :]
        px, py, pz = (jnp.broadcast_to(mom[:, i : i + 1], (LX, 128)) for i in range(3))
        tab[0, k], tab[1, k] = circle((px * index % LX).astype(F32) / LX)
        for core in range(2):
            z = src * slabs + (1 - slab if core else slab)
            fz = (pz * z % lz).astype(F32) / lz
            fy = (py * index % LY).astype(F32) / LY
            tab[2 + 2 * core, k], tab[3 + 2 * core, k] = circle(fy + fz)
    copy.wait()
    tran[...] = vec[...].T
    site_sums(pieces, vec, tab, 0, wide, tran, sums)
    for i in range(len(pieces)):
        acc_ref[i] = sums[i, :nev] + turned(sums[i, nev:], nev)


def same_kernel(pieces, times_hbm, eig_ref, tab, acc_ref, *refs):
    n = len(pieces)
    same = refs[:n]
    wide, rest, times_ref, tran, lhs, sums, sem = refs[n:]
    copy = pltpu.make_async_copy(times_hbm, times_ref, sem)
    copy.start()
    width = eig_ref.shape[2]
    nev = width // 2
    rows = nev // 2
    slab = lax.axis_index("slab")
    vec = eig_ref.at[slab]
    tran[...] = vec[...].T
    for i in range(2):
        lower = tran[i * nev : i * nev + rows, :]
        upper = tran[i * nev + rows : (i + 1) * nev, :]
        lhs[i * rows : (i + 1) * rows, :] = jnp.where(slab == 0, lower, upper)
        rest[i * rows : (i + 1) * rows, :] = jnp.where(slab == 0, upper, lower)
    site_sums(pieces, vec, tab, 1, wide, lhs, sums)
    copy.wait()
    for i, k in enumerate(pieces):
        e = sums[i, :rows] + turned(sums[i, rows:], nev)
        e = e + jnp.where(slab == 0, acc_ref[i, :rows], acc_ref[i, rows:])
        same[i][:rows, :] = e.astype(same[i].dtype)
        if k:
            for s in range(times_ref.shape[1]):
                time = jnp.broadcast_to(times_ref[:, s : s + 1].astype(F32), (TAIL, width))
                same[i][rows + s * TAIL : rows + (s + 1) * TAIL, :] = time.astype(BF16)


def cross_kernel(wide, rest, acc_ref, *outs):
    rows, width = outs[0].shape
    nev = width // 2
    slab = lax.axis_index("slab")
    for i, out in enumerate(outs):
        g = jnp.dot(rest[...], wide[:, i * width : (i + 1) * width], preferred_element_type=F32)
        e = g[:rows] + turned(g[rows:], nev)
        e = e + jnp.where(slab == 0, acc_ref[i, rows:], acc_ref[i, :rows])
        out[...] = e.astype(out.dtype)


def sum_kernel(own, *refs):
    out = refs[-1]
    rows = out.shape[0]
    total = own[...]
    for r in refs[:-1]:
        total = total + r[:rows, :].astype(F32)
    out[...] = total.astype(BF16)


def both_kernel(own, *refs):
    done = refs[-3]
    out, both = refs[-2:]
    total = own[...]
    for r in refs[:-3]:
        total = total + r[...].astype(F32)
    red = total.astype(BF16)
    out[...] = red
    slab = lax.axis_index("slab")
    both[0] = jnp.where(slab == 0, done[...], red)
    both[1] = jnp.where(slab == 0, red, done[...])


def pick_kernel(nsrc, labels, chained, times_ref, *refs):
    n = len(labels)
    sent = refs[: nsrc - 1]
    seen = refs[nsrc - 1 : nsrc - 1 + n]
    before = refs[nsrc - 1 + n : -nsrc]
    outs = refs[-nsrc:]
    rows, width = seen[0].shape[-2:]
    snk = lax.axis_index("snk")
    slab = lax.axis_index("slab")
    for k in range(nsrc):
        for s in range(outs[k].shape[0]):
            if k == 0:
                want = jnp.broadcast_to(times_ref[:, s : s + 1].astype(F32), (TAIL, 128))
            else:
                want = sent[k - 1][rows + s * TAIL : rows + (s + 1) * TAIL, :128].astype(F32)
            mask = []
            for d, other in labels:
                parts = (0, 1) if other is None else (1 - slab if other else slab,)
                for part in parts:
                    time = ((snk ^ d) * 2 + part).astype(F32)
                    one = (want == time).astype(F32).astype(BF16)
                    mask.append(jnp.concatenate([one] * (width // 128), axis=1))
            for r in range(rows // TAIL):
                at = slice(r * TAIL, (r + 1) * TAIL)
                total = before[k][s, at, :] if chained else None
                views = []
                for (_, other), x in zip(labels, seen):
                    views += [x[at, :]] if other is not None else [x[0, at, :], x[1, at, :]]
                for one, x in zip(mask, views):
                    term = one * x
                    total = term if total is None else total + term
                outs[k][s, at, :] = total


def half_kernel(pieces, *refs):
    sinks = refs[:pieces]
    per_ref = refs[pieces]
    outs = refs[pieces + 1 : 2 * pieces + 1]
    lhs, rhs = refs[2 * pieces + 1 :]
    tdev, rows, width = sinks[0].shape
    nev = width // 2
    sdev, nq = per_ref.shape[1:3]
    for t in range(tdev):
        for k in range(pieces):
            lhs[t, k * rows : (k + 1) * rows, :] = sinks[k][t]
        for s in range(sdev):
            for q in range(nq):
                p = per_ref[t, s, q]
                rhs[s, :nev, q * width : (q + 1) * width] = p
                rhs[s, nev:, q * width : (q + 1) * width] = (-turned(p.astype(F32), nev)).astype(BF16)
            h = jnp.dot(lhs[t], rhs[s], preferred_element_type=F32).astype(BF16)
            for q in range(nq):
                for k in range(pieces):
                    part = h[k * rows : (k + 1) * rows, q * width : (q + 1) * width]
                    outs[k][s, t * nq + q] = part


def block_kernel(pieces, chained, *refs):
    n = len(pieces)
    half, mine, other = refs[:n], refs[n : 2 * n], refs[2 * n : 3 * n]
    out_hbm, rhs, buf, sem = refs[3 * n + chained :]
    sdev, rows, width = mine[0].shape
    nev = width // 2
    tdev, nq = buf.shape[1:3]
    slab = lax.axis_index("slab")
    src = lax.axis_index("src")
    copies = []
    for j, k in enumerate(pieces):
        for s in range(sdev):
            slot, part = j * sdev + s, s % 2
            lower = jnp.where(slab == 0, mine[j][s], other[j][s])
            upper = jnp.where(slab == 0, other[j][s], mine[j][s])
            for at, x in ((0, lower), (rows, upper)):
                rhs[part, at : at + rows, :] = x
                rhs[part, nev + at : nev + at + rows, :] = (-turned(x.astype(F32), nev)).astype(BF16)
            for t in range(tdev):
                out = lax.dot_general(
                    half[j][s, t * nq : (t + 1) * nq].reshape(nq * rows, width),
                    rhs[part],
                    (((1,), (1,)), ((), ())),
                    preferred_element_type=F32,
                )
                buf[slot, t] = out.reshape(nq, rows, width)
                copies.append(
                    pltpu.make_async_copy(
                        buf.at[slot, t], out_hbm.at[src ^ k, t, s], sem.at[slot, t]
                    )
                )
                copies[-1].start()
    for copy in copies:
        copy.wait()


def fast(eigvecs, perambulator, momenta, source_times):
    nsrc, nsnk, slabs = (lax.axis_size(a) for a in ("src", "snk", "slab"))
    tdev, count, width = eigvecs.shape
    sdev = source_times.shape[0]
    nq = perambulator.shape[2]
    nev = width // 2
    rows = nev // slabs
    lz = count // (LX * LY) * nsrc * slabs

    def shape(dims, dtype=BF16):
        return jax.ShapeDtypeStruct(dims, dtype)

    def params(mib):
        return pltpu.CompilerParams(vmem_limit_bytes=mib * 2**20)

    def cost(flops, moved):
        return pl.CostEstimate(flops=flops, bytes_accessed=moved, transcendentals=0)

    def swap(x):
        return lax.ppermute(x, "slab", [(0, 1), (1, 0)])

    def cross(x, k):
        return lax.ppermute(x, "src", [(i, i ^ k) for i in range(nsrc)])

    def far(x, k):
        pairs = [(2 * i + j, 2 * (i ^ k) + 1 - j) for i in range(nsrc) for j in range(2)]
        return lax.ppermute(x, ("src", "slab"), pairs)

    def along(x, d):
        return lax.ppermute(x, "snk", [(i, i ^ d) for i in range(nsnk)])

    theirs = swap(eigvecs)
    work = 2 * width * count * width
    hbm = pl.BlockSpec(memory_space=pltpu.HBM)
    sent = list(range(nsrc - 1, -1, -1))

    def grams(n):
        return [
            pltpu.VMEM((count, n * width), BF16),
            pltpu.VMEM((width, count), BF16),
            pltpu.VMEM((n, width, width), F32),
        ]

    vec = pltpu.VMEM((count, width), BF16)
    sem = pltpu.SemaphoreType.DMA

    def held(x):
        return pltpu.with_memory_space_constraint(x, pltpu.HBM)

    eigs = held(eigvecs)
    acc, tab = pl.pallas_call(
        functools.partial(own_kernel, nsrc, slabs, lz, sent),
        out_shape=[shape((len(sent), nev, width), F32), shape((6, nsrc, LX, 128), F32)],
        in_specs=[hbm, hbm],
        out_specs=[VMEM] * 2,
        scratch_shapes=[vec, pltpu.VMEM(momenta.shape, jnp.int32)] + grams(len(sent)) + [sem] * 2,
        cost_estimate=cost(len(sent) * work, 2 * count * width),
        compiler_params=params(12),
        name="gram_own",
    )(held(momenta), eigs)
    parts = pl.pallas_call(
        functools.partial(same_kernel, sent),
        out_shape=[shape((rows + sdev * TAIL, width)) if k else shape((rows, width), F32) for k in sent]
        + [shape((count, nsrc * width)), shape((2 * rows, count))],
        in_specs=[hbm] + [VMEM] * 3,
        out_specs=[VMEM] * (nsrc + 2),
        scratch_shapes=[
            pltpu.VMEM((1, sdev), jnp.int32),
            pltpu.VMEM((width, count), BF16),
            pltpu.VMEM((2 * rows, count), BF16),
            pltpu.VMEM((nsrc, 2 * rows, width), F32),
            sem,
        ],
        cost_estimate=cost(nsrc * work // 2, 2 * count * width),
        compiler_params=params(12),
        name="gram_same",
    )(held(source_times.reshape(1, sdev)), theirs, tab, acc)
    same = dict(zip(sent, parts))
    other = pl.pallas_call(
        cross_kernel,
        out_shape=[shape((rows, width), BF16 if k else F32) for k in sent],
        in_specs=[VMEM] * 3,
        out_specs=[VMEM] * nsrc,
        cost_estimate=cost(nsrc * work // 2, 2 * count * width),
        compiler_params=params(6),
        name="gram_cross",
    )(*parts[nsrc:], acc)
    other = dict(zip(sent, other))
    got = [cross(same[k], k) for k in range(1, nsrc)]
    more = [far(other[k], k) for k in range(1, nsrc)]
    red = pl.pallas_call(
        sum_kernel,
        out_shape=shape((rows, width)),
        in_specs=[VMEM] * nsrc,
        out_specs=VMEM,
        compiler_params=params(4),
        name="sum_same",
    )(same[0], *got)
    red_far, both = pl.pallas_call(
        both_kernel,
        out_shape=[shape((rows, width)), shape((tdev, rows, width))],
        in_specs=[VMEM] * (nsrc + 1),
        out_specs=[VMEM] * 2,
        compiler_params=params(4),
        name="sum_both",
    )(swap(other[0]), *more, red)
    views = {0: {0: red, 1: red_far}}
    seen = [((0, p), x) for p, x in views[0].items()]
    for bit in reversed([1 << i for i in range(nsnk.bit_length() - 1)]):
        for d in sorted(views):
            if bit == 1 and d == 0 and nsnk > 2:
                seen.append(((1, None), along(both, 1)))
                continue
            views[d | bit] = {p: along(x, bit) for p, x in views[d].items()}
            seen += [((d | bit, p), x) for p, x in views[d | bit].items()]
    labels, seen = zip(*seen)
    sinks = [both] + [cross(both, k) for k in range(1, nsrc)]

    def pick(which, before):
        return pl.pallas_call(
            functools.partial(pick_kernel, nsrc, [labels[i] for i in which], bool(before)),
            out_shape=[shape((sdev, rows, width))] * nsrc,
            in_specs=[VMEM] * (nsrc + len(which) + len(before)),
            out_specs=[VMEM] * nsrc,
            compiler_params=params(8),
        )(source_times.reshape(1, sdev), *got, *(seen[i] for i in which), *before)

    late = len(labels) - 1
    picked = pick(list(range(late)), [])
    picked = pick([late], picked)

    tq = tdev * nq

    def halves(which):
        n = len(which)
        out = pl.pallas_call(
            functools.partial(half_kernel, n),
            out_shape=[shape((sdev, tq, rows, width))] * n,
            in_specs=[VMEM] * (n + 1),
            out_specs=[VMEM] * n,
            scratch_shapes=[
                pltpu.VMEM((tdev, n * rows, width), BF16),
                pltpu.VMEM((sdev, width, nq * width), BF16),
            ],
            cost_estimate=cost(2 * tq * sdev * n * rows * width * width, 2 * perambulator.size),
            compiler_params=params(12),
        )(*(sinks[k] for k in which), perambulator)
        return dict(zip(which, out))

    half = halves(list(range(nsrc)))

    mine = [picked[0]] + [cross(picked[k], k) for k in range(1, nsrc)]
    other = [swap(x) for x in mine]

    def finish(which, before):
        n = len(which)
        chained = before is not None
        return pl.pallas_call(
            functools.partial(block_kernel, which, chained),
            out_shape=shape((nsrc, tdev, sdev, nq, rows, width), F32),
            in_specs=[VMEM] * (3 * n) + [hbm] * chained,
            out_specs=hbm,
            scratch_shapes=[
                pltpu.VMEM((2, width, width), BF16),
                pltpu.VMEM((n * sdev, tdev, nq, rows, width), F32),
                pltpu.SemaphoreType.DMA((n * sdev, tdev)),
            ],
            input_output_aliases={3 * n: 0} if chained else {},
            cost_estimate=cost(
                2 * n * tq * sdev * rows * width * width, 4 * n * tq * sdev * rows * width
            ),
            compiler_params=params(16),
        )(
            *(x[k] for x in (half, mine, other) for k in which),
            *([before] if chained else []),
        )

    blocks = finish([0], None)
    return finish(list(range(1, nsrc)), blocks)


def local(eigvecs, perambulator, momenta, source_times):
    nsrc = lax.axis_size("src")
    fits = (
        lax.axis_size("slab") == 2
        and momenta.shape[0] == nsrc
        and nsrc & (nsrc - 1) == 0
        and lax.axis_size("snk") & (lax.axis_size("snk") - 1) == 0
        and eigvecs.shape[0] == 2
        and eigvecs.shape[1] == LX * LY
        and source_times.shape[0] == eigvecs.shape[0]
    )
    return (fast if fits else general)(eigvecs, perambulator, momenta, source_times)


def solution(mesh):
    placed = (P("snk", ("src", "slab"), None), P("snk", "src", None, None, None), P(), P("src"))

    return jax.shard_map(
        local,
        mesh=mesh,
        in_specs=placed,
        out_specs=P(None, "snk", "src", None, "slab", None),
        check_vma=False,
    )
```
